32 devices in a mesh: ty: 4 (over y, core), tx: 8 (over z, x).
Axes of the slice: x: 2, y: 2, z: 4, core: 2. Of those that a mesh axis runs over, the one named last changes fastest.
Arguments:
- object_field: bfloat16 [2, 1024, 2048], P(None, 'ty', 'tx'), may hold values from -5 to 5
- probe_field: float32 [2, 256, 256], replicated, may hold values from -2.1 to 2.1
- corners: int32 [4, 8, 8, 2], P('ty', 'tx'), may hold values from 0 to 255, as said below
- counts: int32 [4, 8], P('ty', 'tx'), may hold values from 0 to 8, as said below
- intensity: bfloat16 [4, 8, 8, 256, 256], P('ty', 'tx'), may hold values from 0 to 1.5
- damping: float32 [], replicated, may hold values from 0.5 to 4
Outputs:
- update: float32 [2, 1024, 2048], P(None, 'ty', 'tx')
The draws below stay inside these ranges and needn't reach their ends.
Inputs may be any that keep to these rules, and one draw needn't show every extreme that they name: `corners`: A patch lies inside the object: on the last tile row (column) of devices the corner's row (column) is 0. A device's live slots are its first counts slots. The counts of the devices of one column (same tx index) sum to exactly 16, and some device of every column holds 8.
All inputs are finite; a program needn't handle non-finite values.
Results may differ from the reference program's by a relative error of at most 0.015.
Values may be sent and summed in bfloat16 or wider, within the bound.
A program may use at most 64 MiB of HBM per device.

```python
import math
import jax
import jax.numpy as jnp
from jax import lax

W = 256
TILE = 256
ITERS = 2
SLOTS = 8
ROW_TILES = 4
COL_TILES = 8
NROW = 1024
NCOL = 2048
POSITIONS = 128


def draw_object_field(key, part):
    amp_key, phase_key = jax.random.split(key)
    row_frac = jnp.arange(NROW, dtype=jnp.float32)[:, None] / NROW
    col_frac = jnp.arange(NCOL, dtype=jnp.float32)[None, :] / NCOL
    slope_ramp = jnp.exp(0.5 * math.log(3.0) * (row_frac + col_frac))
    roughness = jnp.exp(jax.random.uniform(amp_key, (NROW, NCOL), jnp.float32, math.log(0.5), math.log(1.5)))
    phases = jax.random.uniform(phase_key, (NROW, NCOL), jnp.float32, -math.pi, math.pi)
    amplitude = slope_ramp * roughness
    return jnp.stack([amplitude * jnp.cos(phases), amplitude * jnp.sin(phases)], 0).astype(jnp.bfloat16)


def draw_corners(key, part):
    drawn = jax.random.randint(key, (ROW_TILES, COL_TILES, SLOTS, 2), 0, TILE)
    last_row = jnp.arange(ROW_TILES, dtype=jnp.int32)[:, None, None] == ROW_TILES - 1
    last_col = jnp.arange(COL_TILES, dtype=jnp.int32)[None, :, None] == COL_TILES - 1
    row_corner = jnp.where(last_row, jnp.minimum(drawn[..., 0], TILE - W), drawn[..., 0])
    col_corner = jnp.where(last_col, jnp.minimum(drawn[..., 1], TILE - W), drawn[..., 1])
    return jnp.stack([row_corner, col_corner], -1).astype(jnp.int32)


def draw_counts(key, part):
    column_keys = jax.random.split(key, COL_TILES)

    def draw_column(column_key):
        order_key, count_key = jax.random.split(column_key)
        ordering = jax.random.permutation(order_key, ROW_TILES)
        first_counts = jax.random.randint(count_key, (ROW_TILES // 2,), 0, SLOTS + 1)
        first_counts = first_counts.at[0].set(SLOTS)
        paired = jnp.stack([first_counts, SLOTS - first_counts], 1).reshape(-1).astype(jnp.int32)
        return jnp.zeros((ROW_TILES,), jnp.int32).at[ordering].set(paired)
    return jax.vmap(draw_column)(column_keys).T


def block_scale(key, shape, cuts, least, high):
    loudness = 1.0
    for dim, shards_of in cuts:
        draws = jax.random.uniform(jax.random.fold_in(jax.random.fold_in(key, 6), dim), (shards_of,), jnp.float32, least / len(cuts), high / len(cuts))
        loudness = loudness * jnp.repeat(jnp.exp(draws), shape[dim] // shards_of).reshape((-1,) + (1,) * (len(shape) - 1 - dim))
    return loudness


def scatter_about(stream_key, shape, width, bound, kind=jnp.bfloat16):
    entries = width * jax.random.normal(stream_key, shape, jnp.float32)
    return jnp.clip(entries, min=-bound, max=bound).astype(kind)


def setup_inputs(seed: int = 0) -> dict:
    splits = jax.random.split(jax.random.key(seed), 7)
    object_field = draw_object_field(jax.random.fold_in(splits[6], 71), 0)
    probe_field = scatter_about(splits[1], (2, W, W), 0.35, 2.1, jnp.float32)
    corners = draw_corners(jax.random.fold_in(splits[6], 71), 0)
    counts = draw_counts(jax.random.fold_in(splits[6], 71), 0)
    intensity = jnp.clip(1.5 * jax.random.uniform(splits[4], (ROW_TILES, COL_TILES, SLOTS, W, W), jnp.float32) ** block_scale(splits[4], (ROW_TILES, COL_TILES, SLOTS, W, W), ((0, 4), (1, 8)), -0.2, 0.2), 0.0, 1.5).astype(jnp.bfloat16)
    damping = jnp.clip(jnp.exp(jax.random.uniform(splits[5], (), jnp.float32, math.log(0.5), math.log(4.0))), 0.5, 4.0)
    return {"object_field": object_field, "probe_field": probe_field, "corners": corners, "counts": counts, "intensity": intensity, "damping": damping}


def make_table(extent, direction_sign):
    indices = jnp.arange(extent, dtype=jnp.int32)
    phases = ((indices[:, None] * indices[None, :]) % extent).astype(jnp.float32)
    angles = phases * (2.0 * jnp.pi / extent)
    norm_scale = 1.0 / float(extent) ** 0.5
    cosine = jnp.cos(angles) * norm_scale
    sines = direction_sign * jnp.sin(angles) * norm_scale
    tables = jnp.stack([jnp.stack([cosine, sines], 1), jnp.stack([-sines, cosine], 1)], 0)
    return tables.astype(jnp.bfloat16)


def transform(field, tables):
    halfway = jnp.einsum("btrc,tcsk->bsrk", field.astype(jnp.float32), tables.astype(jnp.float32))
    halfway = halfway.astype(jnp.bfloat16)
    return jnp.einsum("btrc,trsk->bskc", halfway.astype(jnp.float32), tables.astype(jnp.float32))


def times_probe(probe_field, patches):
    real_part = probe_field[0] * patches[:, 0] - probe_field[1] * patches[:, 1]
    imag_part = probe_field[0] * patches[:, 1] + probe_field[1] * patches[:, 0]
    return jnp.stack([real_part, imag_part], 1)


def times_conj_probe(probe_field, returned):
    real_part = probe_field[0] * returned[:, 0] + probe_field[1] * returned[:, 1]
    imag_part = probe_field[0] * returned[:, 1] - probe_field[1] * returned[:, 0]
    return jnp.stack([real_part, imag_part], 1)


def reference(object_field, probe_field, corners, counts, intensity, damping):
    extent = probe_field.shape[-1]
    forward = make_table(extent, -1.0)
    inverse = make_table(extent, 1.0)
    slot_ids = jnp.arange(SLOTS, dtype=jnp.int32)
    alive_mask = (slot_ids[None, None, :] < counts[:, :, None]).reshape(-1)
    tile_rows = jnp.arange(ROW_TILES, dtype=jnp.int32)[:, None, None] * TILE
    tile_cols = jnp.arange(COL_TILES, dtype=jnp.int32)[None, :, None] * TILE
    corner_rows = (corners[..., 0] + tile_rows).reshape(-1).astype(jnp.int32)
    corner_cols = (corners[..., 1] + tile_cols).reshape(-1).astype(jnp.int32)
    chosen = jnp.nonzero(alive_mask, size=POSITIONS)[0].astype(jnp.int32)
    corner_rows = corner_rows[chosen]
    corner_cols = corner_cols[chosen]
    measured = intensity.reshape(-1, extent, extent)[chosen]
    group_len = 8
    block_count = POSITIONS // group_len
    block_items = (corner_rows.reshape(block_count, group_len), corner_cols.reshape(block_count, group_len), measured.reshape(block_count, group_len, extent, extent))

    def cut_window(field, row_at, col_at):
        anchor = jnp.zeros((), jnp.int32)
        return lax.dynamic_slice(field, (anchor, row_at, col_at), (2, extent, extent))

    def sweep_all(direction):
        def block_step(totals, items):
            block_rows, block_cols, block_data = items
            patches = jax.vmap(lambda r, c: cut_window(object_field, r, c))(block_rows, block_cols)
            exit_wave = times_probe(probe_field, patches.astype(jnp.float32)).astype(jnp.bfloat16)
            far_field = transform(exit_wave, forward)
            if direction is None:
                powers = far_field[:, 0] * far_field[:, 0] + far_field[:, 1] * far_field[:, 1]
                misfit = powers - block_data.astype(jnp.float32)
                mixture = far_field * misfit[:, None]
                weight_factor = 2.0
            else:
                moved = jax.vmap(lambda r, c: cut_window(direction, r, c))(block_rows, block_cols)
                moved_wave = times_probe(probe_field, moved.astype(jnp.float32)).astype(jnp.bfloat16)
                image_field = transform(moved_wave, forward)
                projected = far_field[:, 0] * image_field[:, 0] + far_field[:, 1] * image_field[:, 1]
                mixture = far_field * projected[:, None]
                weight_factor = 4.0
            returned = transform(mixture.astype(jnp.bfloat16), inverse).astype(jnp.bfloat16)
            contribs = weight_factor * times_conj_probe(probe_field, returned.astype(jnp.float32))

            def add_patch(k, running):
                anchor = jnp.zeros((), jnp.int32)
                previous = lax.dynamic_slice(running, (anchor, block_rows[k], block_cols[k]), (2, extent, extent))
                return lax.dynamic_update_slice(running, previous + contribs[k], (anchor, block_rows[k], block_cols[k]))

            return lax.fori_loop(0, group_len, add_patch, totals), None

        initial = jnp.zeros(object_field.shape, jnp.float32)
        totals, _ = lax.scan(block_step, initial, block_items)
        return totals

    gradient = sweep_all(None)
    residual = -gradient
    direction = residual
    solution = jnp.zeros_like(gradient)
    norm_now = jnp.sum(residual * residual)
    for step in range(ITERS):
        image_field = sweep_all(direction.astype(jnp.bfloat16)) + damping * direction
        step_len = norm_now / jnp.sum(direction * image_field)
        solution = solution + step_len * direction
        residual = residual - step_len * image_field
        norm_next = jnp.sum(residual * residual)
        direction = residual + (norm_next / norm_now) * direction
        norm_now = norm_next
    return solution
```

```python
import functools

import jax
import jax.numpy as jnp
import numpy as np
from jax import lax
from jax.experimental import pallas as pl
from jax.experimental.pallas import tpu as pltpu
from jax.sharding import PartitionSpec as P

MESH = pl.DeviceIdType.MESH
LANES = 128
SCALE = 2.0**-24
F32 = jnp.float32
BF16 = jnp.bfloat16
VMEM_SPEC = pl.BlockSpec(memory_space=pltpu.VMEM)
SMEM_SPEC = pl.BlockSpec(memory_space=pltpu.SMEM)


def make_table(extent, direction_sign):
    indices = np.arange(extent)
    angles = (indices[:, None] * indices[None, :] % extent) * (2.0 * np.pi / extent)
    cosine = np.cos(angles) / extent**0.5
    sines = direction_sign * np.sin(angles) / extent**0.5
    table = np.block([[cosine, sines], [-sines, cosine]])
    return jnp.asarray(table.astype(np.float32)).astype(BF16)


def place():
    ty, tx = lax.axis_index("ty"), lax.axis_index("tx")
    return ty, tx, ty > 0, ty < lax.axis_size("ty") - 1, tx > 0, tx < lax.axis_size("tx") - 1


def greet_neighbours():
    ty, tx, has_up, has_down, has_left, has_right = place()
    barrier = pltpu.get_barrier_semaphore()
    sides = (
        (has_up, {"ty": ty - 1}),
        (has_down, {"ty": ty + 1}),
        (has_left, {"tx": tx - 1}),
        (has_right, {"tx": tx + 1}),
    )
    for present, peer in sides:
        @pl.when(present)
        def _():
            pl.semaphore_signal(barrier, inc=1, device_id=peer, device_id_type=MESH)
    pl.semaphore_wait(barrier, sum(present.astype(jnp.int32) for present, _ in sides))


def remote(src, dst, send_sem, recv_sem, index, peer):
    return pltpu.make_async_remote_copy(
        src_ref=src,
        dst_ref=dst,
        send_sem=send_sem.at[index],
        recv_sem=recv_sem.at[index],
        device_id=peer,
        device_id_type=MESH,
    )


def gather_margins(own, right, below, corner, send_sem, recv_sem, base):
    ty, tx, has_up, has_down, has_left, has_right = place()
    to_left = remote(own, right, send_sem, recv_sem, base, {"tx": tx - 1})
    to_up = remote(own, below, send_sem, recv_sem, base + 1, {"ty": ty - 1})
    on_up = remote(right, corner, send_sem, recv_sem, base + 2, {"ty": ty - 1})

    @pl.when(has_left)
    def _():
        to_left.start()

    @pl.when(has_up)
    def _():
        to_up.start()

    @pl.when(has_right)
    def _():
        to_left.wait_recv()

        @pl.when(has_up)
        def _():
            on_up.start()

    @pl.when(has_down)
    def _():
        to_up.wait_recv()

        @pl.when(has_right)
        def _():
            on_up.wait_recv()

    @pl.when(has_left)
    def _():
        to_left.wait_send()

    @pl.when(has_up)
    def _():
        to_up.wait_send()

        @pl.when(has_right)
        def _():
            on_up.wait_send()


def fold_margins(top, bottom, inbox_far, inbox_near, outbox, inbox_side, total, send_sem, recv_sem):
    ty, tx, has_up, has_down, has_left, has_right = place()
    far = remote(bottom.at[pl.ds(2, 2)], inbox_far, send_sem, recv_sem, 0, {"ty": ty + 1})
    near = remote(bottom.at[pl.ds(0, 2)], inbox_near, send_sem, recv_sem, 1, {"ty": ty + 1})
    side = remote(outbox, inbox_side, send_sem, recv_sem, 2, {"tx": tx + 1})

    @pl.when(has_down)
    def _():
        far.start()
        near.start()

    @pl.when(has_up)
    def _():
        far.wait_recv()

        @pl.when(has_right)
        def _():
            outbox[...] = (top[2:4] + inbox_far[...].astype(F32)).astype(BF16)

    @pl.when(jnp.logical_and(ty == 0, has_right))
    def _():
        outbox[...] = top[2:4].astype(BF16)

    @pl.when(has_right)
    def _():
        side.start()

    @pl.when(has_up)
    def _():
        near.wait_recv()
        total[...] = top[0:2] + inbox_near[...].astype(F32)

    @pl.when(ty == 0)
    def _():
        total[...] = top[0:2]

    @pl.when(has_left)
    def _():
        side.wait_recv()
        total[...] += inbox_side[...].astype(F32)

    @pl.when(has_down)
    def _():
        far.wait_send()
        near.wait_send()

    @pl.when(has_right)
    def _():
        side.wait_send()


def spread_kernel(object_ref, own, right, below, corner, send_sem, recv_sem):
    greet_neighbours()
    for h in range(2):
        for t in range(2):
            own[h, t] = object_ref[t, :, h * LANES:(h + 1) * LANES]
    gather_margins(own, right, below, corner, send_sem, recv_sem, 0)


def exchange_first_kernel(top, bottom, q_ref, own, right, below, corner,
                          inbox_far, inbox_near, outbox, inbox_side, total, send_sem, recv_sem):
    greet_neighbours()
    fold_margins(top, bottom, inbox_far, inbox_near, outbox, inbox_side, total, send_sem, recv_sem)
    q = -2.0 * total[...]
    q_ref[...] = q
    own[...] = q.astype(BF16)
    gather_margins(own, right, below, corner, send_sem, recv_sem, 3)


def exchange_kernel(damping, top, bottom, before, q_ref, own, right, below, corner,
                    inbox_far, inbox_near, outbox, inbox_side, total, send_sem, recv_sem):
    greet_neighbours()
    fold_margins(top, bottom, inbox_far, inbox_near, outbox, inbox_side, total, send_sem, recv_sem)
    q = (4.0 * SCALE) * total[...] + (damping[0] * SCALE) * before[...]
    q_ref[...] = q
    own[...] = q.astype(BF16)
    gather_margins(own, right, below, corner, send_sem, recv_sem, 3)


def lane_sums(values):
    return jnp.sum(values.reshape(-1, LANES), 0, keepdims=True)


def finish_kernel(damping, top, bottom, q0_ref, q1_ref, out_ref,
                  inbox_far, inbox_near, outbox, inbox_side, total, sums_y, sums_x,
                  send_sem, recv_sem, send_y, recv_y, send_x, recv_x):
    ty, tx, has_up, has_down, has_left, has_right = place()
    n_y, n_x = lax.axis_size("ty"), lax.axis_size("tx")
    barrier = pltpu.get_barrier_semaphore()
    for axis, me, n in (("ty", ty, n_y), ("tx", tx, n_x)):
        for step in range(1, n):
            pl.semaphore_signal(
                barrier, inc=1, device_id={axis: lax.rem(me + step, n)}, device_id_type=MESH
            )
    pl.semaphore_wait(barrier, n_y + n_x - 2)
    fold_margins(top, bottom, inbox_far, inbox_near, outbox, inbox_side, total, send_sem, recv_sem)
    q0, q1 = q0_ref[...], q1_ref[...]
    q2 = (4.0 * SCALE) * total[...] + (damping[0] * SCALE) * q1
    rows = [lane_sums(q0 * q0), lane_sums(q0 * q1), lane_sums(q1 * q1), lane_sums(q0 * q2), lane_sums(q1 * q2)]
    partial = jnp.concatenate(rows + [jnp.zeros((3, LANES), F32)], 0)

    def reduce_over(partial, sums, send, recv, axis, me, n):
        sums[me] = partial
        copies = []
        for step in range(1, n):
            copies.append(pltpu.make_async_remote_copy(
                src_ref=sums.at[me], dst_ref=sums.at[me],
                send_sem=send.at[step], recv_sem=recv.at[step],
                device_id={axis: lax.rem(me + step, n)}, device_id_type=MESH,
            ))
        for copy in copies:
            copy.start()
        for copy in copies:
            copy.wait()
        return jnp.sum(sums[...], 0)

    partial = reduce_over(partial, sums_y, send_y, recv_y, "ty", ty, n_y)
    partial = reduce_over(partial, sums_x, send_x, recv_x, "tx", tx, n_x)
    dots = jnp.sum(partial, 1, keepdims=True)
    rr, c01, s11, s02, s12 = (dots[k:k + 1] for k in range(5))
    alpha = rr / c01
    rr_next = rr - 2.0 * alpha * c01 + alpha * alpha * s11
    gain = 1.0 + rr_next / rr
    curvature = gain * gain * c01 - gain * alpha * (s02 + s11) + alpha * alpha * s12
    step_len = rr_next / curvature
    first = (alpha + step_len * gain) * SCALE
    second = step_len * alpha * SCALE
    for h in range(2):
        for t in range(2):
            out_ref[t, :, h * LANES:(h + 1) * LANES] = first * q0_ref[h, t] - second * q1_ref[h, t]


def sweep_kernel(first, group, corners, count, own, right, below, corner, probe, table_f, table_g, extra,
                 top, bottom, *rest):
    if first:
        psi_ref, field, total = rest
    else:
        field, total = rest
        psi_ref = extra
    extent = probe.shape[-1]
    tile = own.shape[2]
    slots = psi_ref.shape[0]
    field[0:2, :, 0:tile] = own[...].astype(F32)
    field[2:4, :, 0:tile] = right[...].astype(F32)
    field[0:2, :, tile:] = below[...].astype(F32)
    field[2:4, :, tile:] = corner[...].astype(F32)
    total[...] = jnp.zeros_like(total)
    lane = lax.broadcasted_iota(jnp.int32, (extent, LANES), 1)
    live = count[0]

    def cut(s):
        row, col = corners[s, 0], corners[s, 1]
        block, shift = col // LANES, lax.rem(col, LANES)
        keep = lane < LANES - shift
        halves = []
        for t in range(2):
            turned = [
                pltpu.roll(field[block + k, t, pl.ds(row, extent), :], lax.rem(LANES - shift, LANES), 1)
                for k in range(3)
            ]
            halves.append([jnp.where(keep, turned[k], turned[k + 1]) for k in range(2)])
        waves = [[], []]
        for k in range(2):
            probe_re = probe[0, :, k * LANES:(k + 1) * LANES]
            probe_im = probe[1, :, k * LANES:(k + 1) * LANES]
            waves[0].append((probe_re * halves[0][k] - probe_im * halves[1][k]).astype(BF16))
            waves[1].append((probe_re * halves[1][k] + probe_im * halves[0][k]).astype(BF16))
        return jnp.concatenate(waves[0] + waves[1], 1)

    def add(s, back):
        row, col = corners[s, 0], corners[s, 1]
        block, shift = col // LANES, lax.rem(col, LANES)
        keep = lane >= shift
        back = back.astype(BF16).astype(F32)
        for t in range(2):
            turned = []
            for k in range(2):
                lanes = slice(k * LANES, (k + 1) * LANES)
                probe_re, probe_im = probe[0, :, lanes], probe[1, :, lanes]
                re, im = back[:extent, lanes], back[extent:, lanes]
                if t == 0:
                    term = probe_re * re + probe_im * im
                else:
                    term = probe_re * im - probe_im * re
                turned.append(pltpu.roll(term, shift, 1))
            zero = jnp.zeros_like(turned[0])
            pieces = [
                jnp.where(keep, turned[0], zero),
                jnp.where(keep, turned[1], turned[0]),
                jnp.where(keep, zero, turned[1]),
            ]
            for k in range(3):
                total[block + k, t, pl.ds(row, extent), :] += pieces[k]

    def transform(waves, rhs, lhs):
        half = jnp.dot(waves, rhs[...], preferred_element_type=F32).astype(BF16)
        columns = []
        for g in range(group):
            part = half[g * extent:(g + 1) * extent]
            columns.append(jnp.concatenate([part[:, :extent], part[:, extent:]], 0))
        return jnp.dot(lhs[...], jnp.concatenate(columns, 1), preferred_element_type=F32)

    def step(index, carry):
        base = index * group
        waves = jnp.concatenate([cut(base + g) for g in range(group)], 0)
        image = transform(waves, table_f, table_g)
        mixed = []
        for g in range(group):
            re = image[:extent, g * extent:(g + 1) * extent]
            im = image[extent:, g * extent:(g + 1) * extent]
            if first:
                psi_ref[base + g, 0] = re
                psi_ref[base + g, 1] = im
                weight = re * re + im * im - extra[base + g].astype(F32)
                psi_re, psi_im = re, im
            else:
                psi_re, psi_im = psi_ref[base + g, 0], psi_ref[base + g, 1]
                weight = psi_re * re + psi_im * im
            mixed.append(jnp.concatenate([(psi_re * weight).astype(BF16), (psi_im * weight).astype(BF16)], 1))
        back = transform(jnp.concatenate(mixed, 0), table_g, table_f)
        for g in range(group):
            @pl.when(base + g < live)
            def _():
                add(base + g, back[:, g * extent:(g + 1) * extent])
        return carry

    lax.fori_loop(0, (live + group - 1) // group, step, 0)
    top[...] = total[:, :, 0:tile]
    bottom[...] = total[:, :, tile:].astype(BF16)


def per_device(object_field, probe_field, corners, counts, intensity, damping):
    extent = probe_field.shape[-1]
    tile = object_field.shape[1]
    slots = corners.shape[2]
    group = 2
    n_y, n_x = lax.axis_size("ty"), lax.axis_size("tx")
    places = corners.reshape(slots, 2)
    count = counts.reshape(1)
    measured = intensity.reshape(slots, extent, extent)
    damping = damping.reshape(1)
    table_f, table_g = make_table(extent, -1.0), make_table(extent, 1.0)

    def shaped(shape, dtype):
        return jax.ShapeDtypeStruct(shape, dtype)

    quarter = (2, 2, tile, LANES)
    quarters = [shaped(quarter, BF16)] * 4
    boxes = [pltpu.VMEM(quarter, BF16)] * 4 + [pltpu.VMEM(quarter, F32)]

    def sems(n):
        return [pltpu.SemaphoreType.DMA((n,)), pltpu.SemaphoreType.DMA((n,))]

    def params(collective_id):
        return pltpu.CompilerParams(
            collective_id=collective_id, has_side_effects=True, vmem_limit_bytes=16 << 20
        )

    margins = pl.pallas_call(
        spread_kernel,
        out_shape=quarters,
        in_specs=[VMEM_SPEC],
        out_specs=[VMEM_SPEC] * 4,
        scratch_shapes=sems(3),
        compiler_params=params(0),
        name="spread",
    )(object_field)

    def sweep(margins, extra, first):
        outs = [shaped((4, 2, tile, LANES), F32), shaped((4, 2, tile, LANES), BF16)]
        if first:
            outs.append(shaped((slots, 2, extent, extent), F32))
        return pl.pallas_call(
            functools.partial(sweep_kernel, first, group),
            out_shape=outs,
            in_specs=[SMEM_SPEC] * 2 + [VMEM_SPEC] * 8,
            out_specs=[VMEM_SPEC] * len(outs),
            scratch_shapes=[pltpu.VMEM((4, 2, 2 * tile, LANES), F32)] * 2,
            compiler_params=pltpu.CompilerParams(vmem_limit_bytes=36 << 20),
            name="sweep_first" if first else "sweep",
        )(places, count, *margins, probe_field, table_f, table_g, extra)

    top, bottom, psi = sweep(margins, measured, True)
    q0, *margins = pl.pallas_call(
        exchange_first_kernel,
        out_shape=[shaped(quarter, F32)] + quarters,
        in_specs=[VMEM_SPEC] * 2,
        out_specs=[VMEM_SPEC] * 5,
        scratch_shapes=boxes + sems(6),
        compiler_params=params(1),
        name="exchange_first",
    )(top, bottom)
    top, bottom = sweep(margins, psi, False)
    q1, *margins = pl.pallas_call(
        exchange_kernel,
        out_shape=[shaped(quarter, F32)] + quarters,
        in_specs=[SMEM_SPEC] + [VMEM_SPEC] * 3,
        out_specs=[VMEM_SPEC] * 5,
        scratch_shapes=boxes + sems(6),
        compiler_params=params(2),
        name="exchange",
    )(damping, top, bottom, q0)
    top, bottom = sweep(margins, psi, False)
    return pl.pallas_call(
        finish_kernel,
        out_shape=shaped((2, tile, tile), F32),
        in_specs=[SMEM_SPEC] + [VMEM_SPEC] * 4,
        out_specs=VMEM_SPEC,
        scratch_shapes=boxes
        + [pltpu.VMEM((n_y, 8, LANES), F32), pltpu.VMEM((n_x, 8, LANES), F32)]
        + sems(3) + sems(n_y) + sems(n_x),
        compiler_params=params(3),
        name="finish",
    )(damping, top, bottom, q0, q1)


def solution(mesh):
    in_specs = (
        P(None, "ty", "tx"),
        P(),
        P("ty", "tx", None, None),
        P("ty", "tx"),
        P("ty", "tx", None, None, None),
        P(),
    )
    out_specs = P(None, "ty", "tx")
    return jax.shard_map(
        per_device, mesh=mesh, in_specs=in_specs, out_specs=out_specs, check_vma=False
    )
```

```python
import functools

import jax
import jax.numpy as jnp
import numpy as np
from jax import lax
from jax.experimental import pallas as pl
from jax.experimental.pallas import tpu as pltpu
from jax.sharding import PartitionSpec as P

MESH = pl.DeviceIdType.MESH
LANES = 128
SCALE = 2.0**-24
CHUNKS = 4
F32 = jnp.float32
BF16 = jnp.bfloat16
VMEM_SPEC = pl.BlockSpec(memory_space=pltpu.VMEM)
SMEM_SPEC = pl.BlockSpec(memory_space=pltpu.SMEM)


def make_table(extent, direction_sign):
    indices = np.arange(extent)
    angles = (indices[:, None] * indices[None, :] % extent) * (2.0 * np.pi / extent)
    cosine = np.cos(angles) / extent**0.5
    sines = direction_sign * np.sin(angles) / extent**0.5
    table = np.block([[cosine, sines], [-sines, cosine]])
    return jnp.asarray(table.astype(np.float32)).astype(BF16)


def place():
    ty, tx = lax.axis_index("ty"), lax.axis_index("tx")
    return ty, tx, ty > 0, ty < lax.axis_size("ty") - 1, tx > 0, tx < lax.axis_size("tx") - 1


def greet_neighbours():
    ty, tx, has_up, has_down, has_left, has_right = place()
    barrier = pltpu.get_barrier_semaphore()
    sides = (
        (has_up, {"ty": ty - 1}),
        (has_down, {"ty": ty + 1}),
        (has_left, {"tx": tx - 1}),
        (has_right, {"tx": tx + 1}),
    )
    for present, peer in sides:
        @pl.when(present)
        def _():
            pl.semaphore_signal(barrier, inc=1, device_id=peer, device_id_type=MESH)
    pl.semaphore_wait(barrier, sum(present.astype(jnp.int32) for present, _ in sides))


def remote(src, dst, send_sem, recv_sem, index, peer):
    return pltpu.make_async_remote_copy(
        src_ref=src,
        dst_ref=dst,
        send_sem=send_sem.at[index],
        recv_sem=recv_sem.at[index],
        device_id=peer,
        device_id_type=MESH,
    )


def rows_of(chunk, extent):
    size = extent // CHUNKS
    return pl.ds(chunk * size, size)


def margin_copies(own, right, below, corner, send_sem, recv_sem, base):
    ty, tx = place()[:2]
    to_left, to_up, on_up = [], [], []
    for c in range(CHUNKS):
        rows = rows_of(c, own.shape[2])
        part = [ref.at[:, :, rows] for ref in (own, right, below, corner)]
        to_left.append(remote(part[0], part[1], send_sem, recv_sem, base + 3 * c, {"tx": tx - 1}))
        to_up.append(remote(part[0], part[2], send_sem, recv_sem, base + 3 * c + 1, {"ty": ty - 1}))
        on_up.append(remote(part[1], part[3], send_sem, recv_sem, base + 3 * c + 2, {"ty": ty - 1}))
    return to_left, to_up, on_up


def send_margins(copies, c):
    ty, tx, has_up, has_down, has_left, has_right = place()
    to_left, to_up, on_up = copies

    @pl.when(has_left)
    def _():
        to_left[c].start()

    @pl.when(has_up)
    def _():
        to_up[c].start()


def settle_margins(copies):
    ty, tx, has_up, has_down, has_left, has_right = place()
    to_left, to_up, on_up = copies

    @pl.when(has_right)
    def _():
        for c in range(CHUNKS):
            to_left[c].wait_recv()

            @pl.when(has_up)
            def _():
                on_up[c].start()

    @pl.when(has_down)
    def _():
        for copy in to_up:
            copy.wait_recv()

        @pl.when(has_right)
        def _():
            for copy in on_up:
                copy.wait_recv()

    @pl.when(has_left)
    def _():
        for copy in to_left:
            copy.wait_send()

    @pl.when(has_up)
    def _():
        for copy in to_up:
            copy.wait_send()

        @pl.when(has_right)
        def _():
            for copy in on_up:
                copy.wait_send()


def fold_margins(top, bottom, inbox_far, inbox_near, outbox, inbox_side, total, send_sem, recv_sem, use):
    ty, tx, has_up, has_down, has_left, has_right = place()
    far, near, side, spans = [], [], [], []
    for c in range(CHUNKS):
        rows = rows_of(c, total.shape[2])
        spans.append(rows)
        far.append(remote(
            bottom.at[pl.ds(2, 2), :, rows], inbox_far.at[:, :, rows], send_sem, recv_sem, 3 * c, {"ty": ty + 1}
        ))
        near.append(remote(
            bottom.at[pl.ds(0, 2), :, rows], inbox_near.at[:, :, rows], send_sem, recv_sem, 3 * c + 1, {"ty": ty + 1}
        ))
        side.append(remote(
            outbox.at[:, :, rows], inbox_side.at[:, :, rows], send_sem, recv_sem, 3 * c + 2, {"tx": tx + 1}
        ))

    @pl.when(has_down)
    def _():
        for copy in far + near:
            copy.start()

    for c in range(CHUNKS):
        @pl.when(has_up)
        def _():
            far[c].wait_recv()

            @pl.when(has_right)
            def _():
                outbox[:, :, spans[c]] = (
                    top[2:4, :, spans[c]] + inbox_far[:, :, spans[c]].astype(F32)
                ).astype(BF16)

        @pl.when(jnp.logical_and(ty == 0, has_right))
        def _():
            outbox[:, :, spans[c]] = top[2:4, :, spans[c]].astype(BF16)

        @pl.when(has_right)
        def _():
            side[c].start()

    for c in range(CHUNKS):
        @pl.when(has_up)
        def _():
            near[c].wait_recv()
            total[:, :, spans[c]] = top[0:2, :, spans[c]] + inbox_near[:, :, spans[c]].astype(F32)

        @pl.when(ty == 0)
        def _():
            total[:, :, spans[c]] = top[0:2, :, spans[c]]

        @pl.when(has_left)
        def _():
            side[c].wait_recv()
            total[:, :, spans[c]] += inbox_side[:, :, spans[c]].astype(F32)

        use(c, spans[c])

    @pl.when(has_down)
    def _():
        for copy in far + near:
            copy.wait_send()

    @pl.when(has_right)
    def _():
        for copy in side:
            copy.wait_send()


def spread_kernel(object_ref, *refs):
    sources, (own, right, below, corner), targets = refs[:4], refs[4:8], refs[8:12]
    send_sem, recv_sem, load_sem = refs[12:]
    loads = [
        pltpu.make_async_copy(
            object_ref.at[t, :, pl.ds(h * LANES, LANES)], own.at[h, t], load_sem.at[2 * h + t]
        )
        for h in range(2) for t in range(2)
    ]
    stages = [
        pltpu.make_async_copy(source, target, load_sem.at[4 + k])
        for k, (source, target) in enumerate(zip(sources, targets))
    ]
    for copy in loads + stages:
        copy.start()
    greet_neighbours()
    for copy in loads:
        copy.wait()
    copies = margin_copies(own, right, below, corner, send_sem, recv_sem, 0)
    for c in range(CHUNKS):
        send_margins(copies, c)
    settle_margins(copies)
    for copy in stages:
        copy.wait()


def exchange_kernel(first, *refs):
    if first:
        top, bottom = refs[:2]
        refs = refs[2:]
    else:
        damping, top, bottom, before = refs[:4]
        refs = refs[4:]
    q_ref, own, right, below, corner = refs[:5]
    boxes, (send_sem, recv_sem) = refs[5:10], refs[10:]
    total = boxes[-1]
    greet_neighbours()
    copies = margin_copies(own, right, below, corner, send_sem, recv_sem, 3 * CHUNKS)

    def use(c, rows):
        if first:
            q = -2.0 * total[:, :, rows]
        else:
            q = (4.0 * SCALE) * total[:, :, rows] + (damping[0] * SCALE) * before[:, :, rows]
        q_ref[:, :, rows] = q
        own[:, :, rows] = q.astype(BF16)
        send_margins(copies, c)

    fold_margins(top, bottom, *boxes, send_sem, recv_sem, use)
    settle_margins(copies)


def lane_sums(values):
    return jnp.sum(values.reshape(-1, LANES), 0, keepdims=True)


def finish_kernel(damping, top, bottom, q0_ref, q1_ref, out_ref,
                  inbox_far, inbox_near, outbox, inbox_side, total, sums_y, sums_x,
                  send_sem, recv_sem, send_y, recv_y, send_x, recv_x):
    ty, tx, has_up, has_down, has_left, has_right = place()
    n_y, n_x = lax.axis_size("ty"), lax.axis_size("tx")
    barrier = pltpu.get_barrier_semaphore()
    for axis, me, n in (("ty", ty, n_y), ("tx", tx, n_x)):
        for step in range(1, n):
            pl.semaphore_signal(
                barrier, inc=1, device_id={axis: lax.rem(me + step, n)}, device_id_type=MESH
            )
    pl.semaphore_wait(barrier, n_y + n_x - 2)
    fold_margins(top, bottom, inbox_far, inbox_near, outbox, inbox_side, total, send_sem, recv_sem,
                 lambda c, rows: None)
    q0, q1 = q0_ref[...], q1_ref[...]
    q2 = (4.0 * SCALE) * total[...] + (damping[0] * SCALE) * q1
    rows = [lane_sums(q0 * q0), lane_sums(q0 * q1), lane_sums(q1 * q1), lane_sums(q0 * q2), lane_sums(q1 * q2)]
    partial = jnp.concatenate(rows + [jnp.zeros((3, LANES), F32)], 0)

    def reduce_over(partial, sums, send, recv, axis, me, n):
        sums[me] = partial
        copies = []
        for step in range(1, n):
            copies.append(pltpu.make_async_remote_copy(
                src_ref=sums.at[me], dst_ref=sums.at[me],
                send_sem=send.at[step], recv_sem=recv.at[step],
                device_id={axis: lax.rem(me + step, n)}, device_id_type=MESH,
            ))
        for copy in copies:
            copy.start()
        for copy in copies:
            copy.wait()
        return jnp.sum(sums[...], 0)

    partial = reduce_over(partial, sums_y, send_y, recv_y, "ty", ty, n_y)
    partial = reduce_over(partial, sums_x, send_x, recv_x, "tx", tx, n_x)
    dots = jnp.sum(partial, 1, keepdims=True)
    rr, c01, s11, s02, s12 = (dots[k:k + 1] for k in range(5))
    alpha = rr / c01
    rr_next = rr - 2.0 * alpha * c01 + alpha * alpha * s11
    gain = 1.0 + rr_next / rr
    curvature = gain * gain * c01 - gain * alpha * (s02 + s11) + alpha * alpha * s12
    step_len = rr_next / curvature
    first = (alpha + step_len * gain) * SCALE
    second = step_len * alpha * SCALE
    for h in range(2):
        for t in range(2):
            out_ref[t, :, h * LANES:(h + 1) * LANES] = first * q0_ref[h, t] - second * q1_ref[h, t]


def sweep_kernel(first, group, corners, count, own, right, below, corner, probe, table_f, table_g, extra,
                 top, bottom, *rest):
    if first:
        psi_ref, field, total = rest
    else:
        field, total = rest
        psi_ref = extra
    extent = probe.shape[-1]
    tile = own.shape[2]
    slots = psi_ref.shape[0]
    field[0:2, :, 0:tile] = own[...].astype(F32)
    field[2:4, :, 0:tile] = right[...].astype(F32)
    field[0:2, :, tile:] = below[...].astype(F32)
    field[2:4, :, tile:] = corner[...].astype(F32)
    total[...] = jnp.zeros_like(total)
    lane = lax.broadcasted_iota(jnp.int32, (extent, LANES), 1)
    live = count[0]

    def cut(s):
        row, col = corners[0, s], corners[1, s]
        block, shift = col // LANES, lax.rem(col, LANES)
        keep = lane < LANES - shift
        halves = []
        for t in range(2):
            turned = [
                pltpu.roll(field[block + k, t, pl.ds(row, extent), :], lax.rem(LANES - shift, LANES), 1)
                for k in range(3)
            ]
            halves.append([jnp.where(keep, turned[k], turned[k + 1]) for k in range(2)])
        waves = [[], []]
        for k in range(2):
            probe_re = probe[0, :, k * LANES:(k + 1) * LANES]
            probe_im = probe[1, :, k * LANES:(k + 1) * LANES]
            waves[0].append((probe_re * halves[0][k] - probe_im * halves[1][k]).astype(BF16))
            waves[1].append((probe_re * halves[1][k] + probe_im * halves[0][k]).astype(BF16))
        return jnp.concatenate(waves[0] + waves[1], 1)

    def add(s, back):
        row, col = corners[0, s], corners[1, s]
        block, shift = col // LANES, lax.rem(col, LANES)
        keep = lane >= shift
        back = back.astype(BF16).astype(F32)
        for t in range(2):
            turned = []
            for k in range(2):
                lanes = slice(k * LANES, (k + 1) * LANES)
                probe_re, probe_im = probe[0, :, lanes], probe[1, :, lanes]
                re, im = back[:extent, lanes], back[extent:, lanes]
                if t == 0:
                    term = probe_re * re + probe_im * im
                else:
                    term = probe_re * im - probe_im * re
                turned.append(pltpu.roll(term, shift, 1))
            zero = jnp.zeros_like(turned[0])
            pieces = [
                jnp.where(keep, turned[0], zero),
                jnp.where(keep, turned[1], turned[0]),
                jnp.where(keep, zero, turned[1]),
            ]
            for k in range(3):
                total[block + k, t, pl.ds(row, extent), :] += pieces[k]

    def transform(waves, rhs, lhs):
        half = jnp.dot(waves, rhs[...], preferred_element_type=F32).astype(BF16)
        columns = []
        for g in range(group):
            part = half[g * extent:(g + 1) * extent]
            columns.append(jnp.concatenate([part[:, :extent], part[:, extent:]], 0))
        return jnp.dot(lhs[...], jnp.concatenate(columns, 1), preferred_element_type=F32)

    def step(index, carry):
        base = index * group
        waves = jnp.concatenate([cut(base + g) for g in range(group)], 0)
        image = transform(waves, table_f, table_g)
        mixed = []
        for g in range(group):
            re = image[:extent, g * extent:(g + 1) * extent]
            im = image[extent:, g * extent:(g + 1) * extent]
            if first:
                psi_ref[base + g, 0] = re
                psi_ref[base + g, 1] = im
                weight = re * re + im * im - extra[base + g].astype(F32)
                psi_re, psi_im = re, im
            else:
                psi_re, psi_im = psi_ref[base + g, 0], psi_ref[base + g, 1]
                weight = psi_re * re + psi_im * im
            mixed.append(jnp.concatenate([(psi_re * weight).astype(BF16), (psi_im * weight).astype(BF16)], 1))
        back = transform(jnp.concatenate(mixed, 0), table_g, table_f)
        for g in range(group):
            @pl.when(base + g < live)
            def _():
                add(base + g, back[:, g * extent:(g + 1) * extent])
        return carry

    lax.fori_loop(0, (live + group - 1) // group, step, 0)
    top[...] = total[:, :, 0:tile]
    bottom[...] = total[:, :, tile:].astype(BF16)


def per_device(object_field, probe_field, corners, counts, intensity, damping):
    extent = probe_field.shape[-1]
    tile = object_field.shape[1]
    slots = corners.shape[2]
    group = 2
    n_y, n_x = lax.axis_size("ty"), lax.axis_size("tx")
    places = corners.reshape(slots, 2).T
    count = counts.reshape(1)
    measured = intensity.reshape(slots, extent, extent)
    damping = damping.reshape(1)
    table_f, table_g = make_table(extent, -1.0), make_table(extent, 1.0)

    def shaped(shape, dtype):
        return jax.ShapeDtypeStruct(shape, dtype)

    quarter = (2, 2, tile, LANES)
    quarters = [shaped(quarter, BF16)] * 4
    boxes = [pltpu.VMEM(quarter, BF16)] * 4 + [pltpu.VMEM(quarter, F32)]

    def sems(n):
        return [pltpu.SemaphoreType.DMA((n,)), pltpu.SemaphoreType.DMA((n,))]

    def params(collective_id):
        return pltpu.CompilerParams(
            collective_id=collective_id, has_side_effects=True, vmem_limit_bytes=16 << 20
        )

    staged = (probe_field, table_f, table_g, measured)
    *margins, probe_field, table_f, table_g, measured = pl.pallas_call(
        spread_kernel,
        out_shape=quarters + [shaped(array.shape, array.dtype) for array in staged],
        in_specs=[pl.BlockSpec(memory_space=pltpu.HBM)] * 5,
        out_specs=[VMEM_SPEC] * 8,
        scratch_shapes=sems(3 * CHUNKS) + [pltpu.SemaphoreType.DMA((8,))],
        compiler_params=params(0),
        name="spread",
    )(object_field, *staged)

    def sweep(margins, extra, first):
        outs = [shaped((4, 2, tile, LANES), F32), shaped((4, 2, tile, LANES), BF16)]
        if first:
            outs.append(shaped((slots, 2, extent, extent), F32))
        return pl.pallas_call(
            functools.partial(sweep_kernel, first, group),
            out_shape=outs,
            in_specs=[SMEM_SPEC] * 2 + [VMEM_SPEC] * 8,
            out_specs=[VMEM_SPEC] * len(outs),
            scratch_shapes=[pltpu.VMEM((4, 2, 2 * tile, LANES), F32)] * 2,
            compiler_params=pltpu.CompilerParams(vmem_limit_bytes=36 << 20),
            name="sweep_first" if first else "sweep",
        )(places, count, *margins, probe_field, table_f, table_g, extra)

    top, bottom, psi = sweep(margins, measured, True)
    q0, *margins = pl.pallas_call(
        functools.partial(exchange_kernel, True),
        out_shape=[shaped(quarter, F32)] + quarters,
        in_specs=[VMEM_SPEC] * 2,
        out_specs=[VMEM_SPEC] * 5,
        scratch_shapes=boxes + sems(6 * CHUNKS),
        compiler_params=params(1),
        name="exchange_first",
    )(top, bottom)
    top, bottom = sweep(margins, psi, False)
    q1, *margins = pl.pallas_call(
        functools.partial(exchange_kernel, False),
        out_shape=[shaped(quarter, F32)] + quarters,
        in_specs=[SMEM_SPEC] + [VMEM_SPEC] * 3,
        out_specs=[VMEM_SPEC] * 5,
        scratch_shapes=boxes + sems(6 * CHUNKS),
        compiler_params=params(2),
        name="exchange",
    )(damping, top, bottom, q0)
    top, bottom = sweep(margins, psi, False)
    return pl.pallas_call(
        finish_kernel,
        out_shape=shaped((2, tile, tile), F32),
        in_specs=[SMEM_SPEC] + [VMEM_SPEC] * 4,
        out_specs=VMEM_SPEC,
        scratch_shapes=boxes
        + [pltpu.VMEM((n_y, 8, LANES), F32), pltpu.VMEM((n_x, 8, LANES), F32)]
        + sems(3 * CHUNKS) + sems(n_y) + sems(n_x),
        compiler_params=params(3),
        name="finish",
    )(damping, top, bottom, q0, q1)


def solution(mesh):
    in_specs = (
        P(None, "ty", "tx"),
        P(),
        P("ty", "tx", None, None),
        P("ty", "tx"),
        P("ty", "tx", None, None, None),
        P(),
    )
    out_specs = P(None, "ty", "tx")
    return jax.shard_map(
        per_device, mesh=mesh, in_specs=in_specs, out_specs=out_specs, check_vma=False
    )
```

```python
import functools

import jax
import jax.numpy as jnp
import numpy as np
from jax import lax
from jax.experimental import pallas as pl
from jax.experimental.pallas import tpu as pltpu
from jax.sharding import PartitionSpec as P

MESH = pl.DeviceIdType.MESH
LANES = 128
SCALE = 2.0**-24
CHUNKS = 4
F32 = jnp.float32
BF16 = jnp.bfloat16
VMEM_SPEC = pl.BlockSpec(memory_space=pltpu.VMEM)
SMEM_SPEC = pl.BlockSpec(memory_space=pltpu.SMEM)


def make_table(extent, direction_sign):
    indices = np.arange(extent)
    angles = (indices[:, None] * indices[None, :] % extent) * (2.0 * np.pi / extent)
    cosine = np.cos(angles) / extent**0.5
    sines = direction_sign * np.sin(angles) / extent**0.5
    table = np.block([[cosine, sines], [-sines, cosine]])
    return jnp.asarray(table.astype(np.float32)).astype(BF16)


def place():
    ty, tx = lax.axis_index("ty"), lax.axis_index("tx")
    return ty, tx, ty > 0, ty < lax.axis_size("ty") - 1, tx > 0, tx < lax.axis_size("tx") - 1


def greet_neighbours():
    ty, tx, has_up, has_down, has_left, has_right = place()
    barrier = pltpu.get_barrier_semaphore()
    sides = (
        (has_up, {"ty": ty - 1}),
        (has_down, {"ty": ty + 1}),
        (has_left, {"tx": tx - 1}),
        (has_right, {"tx": tx + 1}),
    )
    for present, peer in sides:
        @pl.when(present)
        def _():
            pl.semaphore_signal(barrier, inc=1, device_id=peer, device_id_type=MESH)
    pl.semaphore_wait(barrier, sum(present.astype(jnp.int32) for present, _ in sides))


def remote(src, dst, send_sem, recv_sem, index, peer):
    return pltpu.make_async_remote_copy(
        src_ref=src,
        dst_ref=dst,
        send_sem=send_sem.at[index],
        recv_sem=recv_sem.at[index],
        device_id=peer,
        device_id_type=MESH,
    )


def rows_of(chunk, extent):
    size = extent // CHUNKS
    return pl.ds(chunk * size, size)


def margin_copies(own, right, below, corner, send_sem, recv_sem, base):
    ty, tx = place()[:2]
    to_left, to_up, on_up = [], [], []
    for c in range(CHUNKS):
        rows = rows_of(c, own.shape[2])
        part = [ref.at[:, :, rows] for ref in (own, right, below, corner)]
        to_left.append(remote(part[0], part[1], send_sem, recv_sem, base + 3 * c, {"tx": tx - 1}))
        to_up.append(remote(part[0], part[2], send_sem, recv_sem, base + 3 * c + 1, {"ty": ty - 1}))
        on_up.append(remote(part[1], part[3], send_sem, recv_sem, base + 3 * c + 2, {"ty": ty - 1}))
    return to_left, to_up, on_up


def send_margins(copies, c):
    ty, tx, has_up, has_down, has_left, has_right = place()
    to_left, to_up, on_up = copies

    @pl.when(has_left)
    def _():
        to_left[c].start()

    @pl.when(has_up)
    def _():
        to_up[c].start()


def settle_margins(copies):
    ty, tx, has_up, has_down, has_left, has_right = place()
    to_left, to_up, on_up = copies

    @pl.when(has_right)
    def _():
        for c in range(CHUNKS):
            to_left[c].wait_recv()

            @pl.when(has_up)
            def _():
                on_up[c].start()

    @pl.when(has_down)
    def _():
        for copy in to_up:
            copy.wait_recv()

        @pl.when(has_right)
        def _():
            for copy in on_up:
                copy.wait_recv()

    @pl.when(has_left)
    def _():
        for copy in to_left:
            copy.wait_send()

    @pl.when(has_up)
    def _():
        for copy in to_up:
            copy.wait_send()

        @pl.when(has_right)
        def _():
            for copy in on_up:
                copy.wait_send()


def fold_margins(top, bottom, inbox_far, inbox_near, outbox, inbox_side, total, send_sem, recv_sem, use):
    ty, tx, has_up, has_down, has_left, has_right = place()
    far, near, side, spans = [], [], [], []
    for c in range(CHUNKS):
        rows = rows_of(c, total.shape[2])
        spans.append(rows)
        far.append(remote(
            bottom.at[pl.ds(2, 2), :, rows], inbox_far.at[:, :, rows], send_sem, recv_sem, 3 * c, {"ty": ty + 1}
        ))
        near.append(remote(
            bottom.at[pl.ds(0, 2), :, rows], inbox_near.at[:, :, rows], send_sem, recv_sem, 3 * c + 1, {"ty": ty + 1}
        ))
        side.append(remote(
            outbox.at[:, :, rows], inbox_side.at[:, :, rows], send_sem, recv_sem, 3 * c + 2, {"tx": tx + 1}
        ))

    @pl.when(has_down)
    def _():
        for copy in far + near:
            copy.start()

    for c in range(CHUNKS):
        @pl.when(has_up)
        def _():
            far[c].wait_recv()

            @pl.when(has_right)
            def _():
                outbox[:, :, spans[c]] = (
                    top[2:4, :, spans[c]] + inbox_far[:, :, spans[c]].astype(F32)
                ).astype(BF16)

        @pl.when(jnp.logical_and(ty == 0, has_right))
        def _():
            outbox[:, :, spans[c]] = top[2:4, :, spans[c]].astype(BF16)

        @pl.when(has_right)
        def _():
            side[c].start()

    for c in range(CHUNKS):
        @pl.when(has_up)
        def _():
            near[c].wait_recv()
            total[:, :, spans[c]] = top[0:2, :, spans[c]] + inbox_near[:, :, spans[c]].astype(F32)

        @pl.when(ty == 0)
        def _():
            total[:, :, spans[c]] = top[0:2, :, spans[c]]

        @pl.when(has_left)
        def _():
            side[c].wait_recv()
            total[:, :, spans[c]] += inbox_side[:, :, spans[c]].astype(F32)

        use(c, spans[c])

    @pl.when(has_down)
    def _():
        for copy in far + near:
            copy.wait_send()

    @pl.when(has_right)
    def _():
        for copy in side:
            copy.wait_send()


def spread_kernel(object_ref, own, right, below, corner, send_sem, recv_sem):
    for h in range(2):
        for t in range(2):
            own[h, t] = object_ref[t, :, h * LANES:(h + 1) * LANES]
    greet_neighbours()
    copies = margin_copies(own, right, below, corner, send_sem, recv_sem, 0)
    for c in range(CHUNKS):
        send_margins(copies, c)
    settle_margins(copies)


def exchange_kernel(first, *refs):
    if first:
        top, bottom = refs[:2]
        refs = refs[2:]
    else:
        damping, top, bottom, before = refs[:4]
        refs = refs[4:]
    q_ref, own, right, below, corner = refs[:5]
    boxes, (send_sem, recv_sem) = refs[5:10], refs[10:]
    total = boxes[-1]
    greet_neighbours()
    copies = margin_copies(own, right, below, corner, send_sem, recv_sem, 3 * CHUNKS)

    def use(c, rows):
        if first:
            q = -2.0 * total[:, :, rows]
        else:
            q = (4.0 * SCALE) * total[:, :, rows] + (damping[0] * SCALE) * before[:, :, rows]
        q_ref[:, :, rows] = q
        own[:, :, rows] = q.astype(BF16)
        send_margins(copies, c)

    fold_margins(top, bottom, *boxes, send_sem, recv_sem, use)
    settle_margins(copies)


def lane_sums(values):
    return jnp.sum(values.reshape(-1, LANES), 0, keepdims=True)


def finish_kernel(damping, top, bottom, q0_ref, q1_ref, out_ref,
                  inbox_far, inbox_near, outbox, inbox_side, total, sums_y, sums_x,
                  send_sem, recv_sem, send_y, recv_y, send_x, recv_x):
    ty, tx, has_up, has_down, has_left, has_right = place()
    n_y, n_x = lax.axis_size("ty"), lax.axis_size("tx")
    barrier = pltpu.get_barrier_semaphore()
    for axis, me, n in (("ty", ty, n_y), ("tx", tx, n_x)):
        for step in range(1, n):
            pl.semaphore_signal(
                barrier, inc=1, device_id={axis: lax.rem(me + step, n)}, device_id_type=MESH
            )
    pl.semaphore_wait(barrier, n_y + n_x - 2)
    fold_margins(top, bottom, inbox_far, inbox_near, outbox, inbox_side, total, send_sem, recv_sem,
                 lambda c, rows: None)
    q0, q1 = q0_ref[...], q1_ref[...]
    q2 = (4.0 * SCALE) * total[...] + (damping[0] * SCALE) * q1
    rows = [lane_sums(q0 * q0), lane_sums(q0 * q1), lane_sums(q1 * q1), lane_sums(q0 * q2), lane_sums(q1 * q2)]
    partial = jnp.concatenate(rows + [jnp.zeros((3, LANES), F32)], 0)

    def reduce_over(partial, sums, send, recv, axis, me, n):
        sums[me] = partial
        copies = []
        for step in range(1, n):
            copies.append(pltpu.make_async_remote_copy(
                src_ref=sums.at[me], dst_ref=sums.at[me],
                send_sem=send.at[step], recv_sem=recv.at[step],
                device_id={axis: lax.rem(me + step, n)}, device_id_type=MESH,
            ))
        for copy in copies:
            copy.start()
        for copy in copies:
            copy.wait()
        return jnp.sum(sums[...], 0)

    partial = reduce_over(partial, sums_y, send_y, recv_y, "ty", ty, n_y)
    partial = reduce_over(partial, sums_x, send_x, recv_x, "tx", tx, n_x)
    dots = jnp.sum(partial, 1, keepdims=True)
    rr, c01, s11, s02, s12 = (dots[k:k + 1] for k in range(5))
    alpha = rr / c01
    rr_next = rr - 2.0 * alpha * c01 + alpha * alpha * s11
    gain = 1.0 + rr_next / rr
    curvature = gain * gain * c01 - gain * alpha * (s02 + s11) + alpha * alpha * s12
    step_len = rr_next / curvature
    first = (alpha + step_len * gain) * SCALE
    second = step_len * alpha * SCALE
    for h in range(2):
        for t in range(2):
            out_ref[t, :, h * LANES:(h + 1) * LANES] = first * q0_ref[h, t] - second * q1_ref[h, t]


def sweep_kernel(first, group, corners, count, own, right, below, corner, probe, table_f, table_g, extra,
                 top, bottom, *rest):
    if first:
        psi_ref, field, total = rest
    else:
        field, total = rest
        psi_ref = extra
    extent = probe.shape[-1]
    tile = own.shape[2]
    slots = psi_ref.shape[0]
    field[0:2, :, 0:tile] = own[...].astype(F32)
    field[2:4, :, 0:tile] = right[...].astype(F32)
    field[0:2, :, tile:] = below[...].astype(F32)
    field[2:4, :, tile:] = corner[...].astype(F32)
    total[...] = jnp.zeros_like(total)
    lane = lax.broadcasted_iota(jnp.int32, (extent, LANES), 1)
    live = count[0]

    def cut(s):
        row, col = corners[0, s], corners[1, s]
        block, shift = col // LANES, lax.rem(col, LANES)
        keep = lane < LANES - shift
        halves = []
        for t in range(2):
            turned = [
                pltpu.roll(field[block + k, t, pl.ds(row, extent), :], lax.rem(LANES - shift, LANES), 1)
                for k in range(3)
            ]
            halves.append([jnp.where(keep, turned[k], turned[k + 1]) for k in range(2)])
        waves = [[], []]
        for k in range(2):
            probe_re = probe[0, :, k * LANES:(k + 1) * LANES]
            probe_im = probe[1, :, k * LANES:(k + 1) * LANES]
            waves[0].append((probe_re * halves[0][k] - probe_im * halves[1][k]).astype(BF16))
            waves[1].append((probe_re * halves[1][k] + probe_im * halves[0][k]).astype(BF16))
        return jnp.concatenate(waves[0] + waves[1], 1)

    def add(s, back):
        row, col = corners[0, s], corners[1, s]
        block, shift = col // LANES, lax.rem(col, LANES)
        keep = lane >= shift
        back = back.astype(BF16).astype(F32)
        for t in range(2):
            turned = []
            for k in range(2):
                lanes = slice(k * LANES, (k + 1) * LANES)
                probe_re, probe_im = probe[0, :, lanes], probe[1, :, lanes]
                re, im = back[:extent, lanes], back[extent:, lanes]
                if t == 0:
                    term = probe_re * re + probe_im * im
                else:
                    term = probe_re * im - probe_im * re
                turned.append(pltpu.roll(term, shift, 1))
            zero = jnp.zeros_like(turned[0])
            pieces = [
                jnp.where(keep, turned[0], zero),
                jnp.where(keep, turned[1], turned[0]),
                jnp.where(keep, zero, turned[1]),
            ]
            for k in range(3):
                total[block + k, t, pl.ds(row, extent), :] += pieces[k]

    def transform(waves, rhs, lhs):
        half = jnp.dot(waves, rhs[...], preferred_element_type=F32).astype(BF16)
        columns = []
        for g in range(group):
            part = half[g * extent:(g + 1) * extent]
            columns.append(jnp.concatenate([part[:, :extent], part[:, extent:]], 0))
        return jnp.dot(lhs[...], jnp.concatenate(columns, 1), preferred_element_type=F32)

    def step(index, carry):
        base = index * group
        waves = jnp.concatenate([cut(base + g) for g in range(group)], 0)
        image = transform(waves, table_f, table_g)
        mixed = []
        for g in range(group):
            re = image[:extent, g * extent:(g + 1) * extent]
            im = image[extent:, g * extent:(g + 1) * extent]
            if first:
                psi_ref[base + g, 0] = re
                psi_ref[base + g, 1] = im
                weight = re * re + im * im - extra[base + g].astype(F32)
                psi_re, psi_im = re, im
            else:
                psi_re, psi_im = psi_ref[base + g, 0], psi_ref[base + g, 1]
                weight = psi_re * re + psi_im * im
            mixed.append(jnp.concatenate([(psi_re * weight).astype(BF16), (psi_im * weight).astype(BF16)], 1))
        back = transform(jnp.concatenate(mixed, 0), table_g, table_f)
        for g in range(group):
            @pl.when(base + g < live)
            def _():
                add(base + g, back[:, g * extent:(g + 1) * extent])
        return carry

    lax.fori_loop(0, (live + group - 1) // group, step, 0)
    top[...] = total[:, :, 0:tile]
    bottom[...] = total[:, :, tile:].astype(BF16)


def per_device(object_field, probe_field, corners, counts, intensity, damping):
    extent = probe_field.shape[-1]
    tile = object_field.shape[1]
    slots = corners.shape[2]
    group = min(4, slots)
    n_y, n_x = lax.axis_size("ty"), lax.axis_size("tx")
    places = corners.reshape(slots, 2).T
    count = counts.reshape(1)
    measured = intensity.reshape(slots, extent, extent)
    damping = damping.reshape(1)
    table_f, table_g = make_table(extent, -1.0), make_table(extent, 1.0)

    def shaped(shape, dtype):
        return jax.ShapeDtypeStruct(shape, dtype)

    quarter = (2, 2, tile, LANES)
    quarters = [shaped(quarter, BF16)] * 4
    boxes = [pltpu.VMEM(quarter, BF16)] * 4 + [pltpu.VMEM(quarter, F32)]

    def sems(n):
        return [pltpu.SemaphoreType.DMA((n,)), pltpu.SemaphoreType.DMA((n,))]

    def params(collective_id):
        return pltpu.CompilerParams(
            collective_id=collective_id, has_side_effects=True, vmem_limit_bytes=16 << 20
        )

    margins = pl.pallas_call(
        spread_kernel,
        out_shape=quarters,
        in_specs=[VMEM_SPEC],
        out_specs=[VMEM_SPEC] * 4,
        scratch_shapes=sems(3 * CHUNKS),
        compiler_params=params(0),
        cost_estimate=pl.CostEstimate(flops=10**10, bytes_accessed=30 << 20, transcendentals=0),
        name="spread",
    )(object_field)

    def sweep(margins, extra, first):
        outs = [shaped((4, 2, tile, LANES), F32), shaped((4, 2, tile, LANES), BF16)]
        if first:
            outs.append(shaped((slots, 2, extent, extent), F32))
        return pl.pallas_call(
            functools.partial(sweep_kernel, first, group),
            out_shape=outs,
            in_specs=[SMEM_SPEC] * 2 + [VMEM_SPEC] * 8,
            out_specs=[VMEM_SPEC] * len(outs),
            scratch_shapes=[pltpu.VMEM((4, 2, 2 * tile, LANES), F32)] * 2,
            compiler_params=pltpu.CompilerParams(vmem_limit_bytes=36 << 20),
            name="sweep_first" if first else "sweep",
        )(places, count, *margins, probe_field, table_f, table_g, extra)

    top, bottom, psi = sweep(margins, measured, True)
    q0, *margins = pl.pallas_call(
        functools.partial(exchange_kernel, True),
        out_shape=[shaped(quarter, F32)] + quarters,
        in_specs=[VMEM_SPEC] * 2,
        out_specs=[VMEM_SPEC] * 5,
        scratch_shapes=boxes + sems(6 * CHUNKS),
        compiler_params=params(1),
        name="exchange_first",
    )(top, bottom)
    top, bottom = sweep(margins, psi, False)
    q1, *margins = pl.pallas_call(
        functools.partial(exchange_kernel, False),
        out_shape=[shaped(quarter, F32)] + quarters,
        in_specs=[SMEM_SPEC] + [VMEM_SPEC] * 3,
        out_specs=[VMEM_SPEC] * 5,
        scratch_shapes=boxes + sems(6 * CHUNKS),
        compiler_params=params(2),
        name="exchange",
    )(damping, top, bottom, q0)
    top, bottom = sweep(margins, psi, False)
    return pl.pallas_call(
        finish_kernel,
        out_shape=shaped((2, tile, tile), F32),
        in_specs=[SMEM_SPEC] + [VMEM_SPEC] * 4,
        out_specs=VMEM_SPEC,
        scratch_shapes=boxes
        + [pltpu.VMEM((n_y, 8, LANES), F32), pltpu.VMEM((n_x, 8, LANES), F32)]
        + sems(3 * CHUNKS) + sems(n_y) + sems(n_x),
        compiler_params=params(3),
        name="finish",
    )(damping, top, bottom, q0, q1)


def solution(mesh):
    in_specs = (
        P(None, "ty", "tx"),
        P(),
        P("ty", "tx", None, None),
        P("ty", "tx"),
        P("ty", "tx", None, None, None),
        P(),
    )
    out_specs = P(None, "ty", "tx")
    return jax.shard_map(
        per_device, mesh=mesh, in_specs=in_specs, out_specs=out_specs, check_vma=False
    )
```

```python
import functools

import jax
import jax.numpy as jnp
import numpy as np
from jax import lax
from jax.experimental import pallas as pl
from jax.experimental.pallas import tpu as pltpu
from jax.sharding import PartitionSpec as P

MESH = pl.DeviceIdType.MESH
LANES = 128
SCALE = 2.0**-24
CHUNKS = 4
F32 = jnp.float32
BF16 = jnp.bfloat16
VMEM_SPEC = pl.BlockSpec(memory_space=pltpu.VMEM)
SMEM_SPEC = pl.BlockSpec(memory_space=pltpu.SMEM)


def make_table(extent, direction_sign):
    indices = np.arange(extent)
    angles = (indices[:, None] * indices[None, :] % extent) * (2.0 * np.pi / extent)
    cosine = np.cos(angles) / extent**0.5
    sines = direction_sign * np.sin(angles) / extent**0.5
    table = np.block([[cosine, sines], [-sines, cosine]])
    return jnp.asarray(table.astype(np.float32)).astype(BF16)


def place():
    ty, tx = lax.axis_index("ty"), lax.axis_index("tx")
    return ty, tx, ty > 0, ty < lax.axis_size("ty") - 1, tx > 0, tx < lax.axis_size("tx") - 1


def greet_neighbours():
    ty, tx, has_up, has_down, has_left, has_right = place()
    barrier = pltpu.get_barrier_semaphore()
    sides = (
        (has_up, {"ty": ty - 1}),
        (has_down, {"ty": ty + 1}),
        (has_left, {"tx": tx - 1}),
        (has_right, {"tx": tx + 1}),
    )
    for present, peer in sides:
        @pl.when(present)
        def _():
            pl.semaphore_signal(barrier, inc=1, device_id=peer, device_id_type=MESH)
    pl.semaphore_wait(barrier, sum(present.astype(jnp.int32) for present, _ in sides))


def remote(src, dst, send_sem, recv_sem, index, peer):
    return pltpu.make_async_remote_copy(
        src_ref=src,
        dst_ref=dst,
        send_sem=send_sem.at[index],
        recv_sem=recv_sem.at[index],
        device_id=peer,
        device_id_type=MESH,
    )


def rows_of(chunk, extent):
    size = extent // CHUNKS
    return pl.ds(chunk * size, size)


def margin_copies(own, right, below, corner, send_sem, recv_sem, base):
    ty, tx = place()[:2]
    to_left, to_up, on_up = [], [], []
    for c in range(CHUNKS):
        rows = rows_of(c, own.shape[2])
        part = [ref.at[:, :, rows] for ref in (own, right, below, corner)]
        to_left.append(remote(part[0], part[1], send_sem, recv_sem, base + 3 * c, {"tx": tx - 1}))
        to_up.append(remote(part[0], part[2], send_sem, recv_sem, base + 3 * c + 1, {"ty": ty - 1}))
        on_up.append(remote(part[1], part[3], send_sem, recv_sem, base + 3 * c + 2, {"ty": ty - 1}))
    return to_left, to_up, on_up


def send_margins(copies, c):
    ty, tx, has_up, has_down, has_left, has_right = place()
    to_left, to_up, on_up = copies

    @pl.when(has_left)
    def _():
        to_left[c].start()

    @pl.when(has_up)
    def _():
        to_up[c].start()


def settle_margins(copies):
    ty, tx, has_up, has_down, has_left, has_right = place()
    to_left, to_up, on_up = copies

    @pl.when(has_right)
    def _():
        for c in range(CHUNKS):
            to_left[c].wait_recv()

            @pl.when(has_up)
            def _():
                on_up[c].start()

    @pl.when(has_down)
    def _():
        for copy in to_up:
            copy.wait_recv()

        @pl.when(has_right)
        def _():
            for copy in on_up:
                copy.wait_recv()

    @pl.when(has_left)
    def _():
        for copy in to_left:
            copy.wait_send()

    @pl.when(has_up)
    def _():
        for copy in to_up:
            copy.wait_send()

        @pl.when(has_right)
        def _():
            for copy in on_up:
                copy.wait_send()


def fold_margins(top, bottom, inbox_far, inbox_near, outbox, inbox_side, total, send_sem, recv_sem, use):
    ty, tx, has_up, has_down, has_left, has_right = place()
    far, near, side, spans = [], [], [], []
    for c in range(CHUNKS):
        rows = rows_of(c, total.shape[2])
        spans.append(rows)
        far.append(remote(
            bottom.at[pl.ds(2, 2), :, rows], inbox_far.at[:, :, rows], send_sem, recv_sem, 3 * c, {"ty": ty + 1}
        ))
        near.append(remote(
            bottom.at[pl.ds(0, 2), :, rows], inbox_near.at[:, :, rows], send_sem, recv_sem, 3 * c + 1, {"ty": ty + 1}
        ))
        side.append(remote(
            outbox.at[:, :, rows], inbox_side.at[:, :, rows], send_sem, recv_sem, 3 * c + 2, {"tx": tx + 1}
        ))

    @pl.when(has_down)
    def _():
        for copy in far + near:
            copy.start()

    for c in range(CHUNKS):
        @pl.when(has_up)
        def _():
            far[c].wait_recv()

            @pl.when(has_right)
            def _():
                outbox[:, :, spans[c]] = (
                    top[2:4, :, spans[c]] + inbox_far[:, :, spans[c]].astype(F32)
                ).astype(BF16)

        @pl.when(jnp.logical_and(ty == 0, has_right))
        def _():
            outbox[:, :, spans[c]] = top[2:4, :, spans[c]].astype(BF16)

        @pl.when(has_right)
        def _():
            side[c].start()

    for c in range(CHUNKS):
        @pl.when(has_up)
        def _():
            near[c].wait_recv()
            total[:, :, spans[c]] = top[0:2, :, spans[c]] + inbox_near[:, :, spans[c]].astype(F32)

        @pl.when(ty == 0)
        def _():
            total[:, :, spans[c]] = top[0:2, :, spans[c]]

        @pl.when(has_left)
        def _():
            side[c].wait_recv()
            total[:, :, spans[c]] += inbox_side[:, :, spans[c]].astype(F32)

        use(c, spans[c])

    @pl.when(has_down)
    def _():
        for copy in far + near:
            copy.wait_send()

    @pl.when(has_right)
    def _():
        for copy in side:
            copy.wait_send()


def spread_kernel(object_ref, own, right, below, corner, send_sem, recv_sem):
    for h in range(2):
        for t in range(2):
            own[h, t] = object_ref[t, :, h * LANES:(h + 1) * LANES]
    greet_neighbours()
    copies = margin_copies(own, right, below, corner, send_sem, recv_sem, 0)
    for c in range(CHUNKS):
        send_margins(copies, c)
    settle_margins(copies)


def exchange_kernel(first, *refs):
    if first:
        top, bottom = refs[:2]
        refs = refs[2:]
    else:
        damping, top, bottom, before = refs[:4]
        refs = refs[4:]
    q_ref, own, right, below, corner = refs[:5]
    boxes, (send_sem, recv_sem) = refs[5:10], refs[10:]
    total = boxes[-1]
    greet_neighbours()
    copies = margin_copies(own, right, below, corner, send_sem, recv_sem, 3 * CHUNKS)

    def use(c, rows):
        if first:
            q = -2.0 * total[:, :, rows]
        else:
            q = (4.0 * SCALE) * total[:, :, rows] + (damping[0] * SCALE) * before[:, :, rows]
        q_ref[:, :, rows] = q
        own[:, :, rows] = q.astype(BF16)
        send_margins(copies, c)

    fold_margins(top, bottom, *boxes, send_sem, recv_sem, use)
    settle_margins(copies)


def lane_sums(values):
    return jnp.sum(values.reshape(-1, LANES), 0, keepdims=True)


def finish_kernel(damping, top, bottom, q0_ref, q1_ref, out_ref,
                  inbox_far, inbox_near, outbox, inbox_side, total, sums_y, sums_x,
                  send_sem, recv_sem, send_y, recv_y, send_x, recv_x):
    ty, tx, has_up, has_down, has_left, has_right = place()
    n_y, n_x = lax.axis_size("ty"), lax.axis_size("tx")
    barrier = pltpu.get_barrier_semaphore()
    for axis, me, n in (("ty", ty, n_y), ("tx", tx, n_x)):
        for step in range(1, n):
            pl.semaphore_signal(
                barrier, inc=1, device_id={axis: lax.rem(me + step, n)}, device_id_type=MESH
            )
    pl.semaphore_wait(barrier, n_y + n_x - 2)
    fold_margins(top, bottom, inbox_far, inbox_near, outbox, inbox_side, total, send_sem, recv_sem,
                 lambda c, rows: None)
    q0, q1 = q0_ref[...], q1_ref[...]
    q2 = (4.0 * SCALE) * total[...] + (damping[0] * SCALE) * q1
    rows = [lane_sums(q0 * q0), lane_sums(q0 * q1), lane_sums(q1 * q1), lane_sums(q0 * q2), lane_sums(q1 * q2)]
    partial = jnp.concatenate(rows + [jnp.zeros((3, LANES), F32)], 0)

    def reduce_over(partial, sums, send, recv, axis, me, n):
        sums[me] = partial
        copies = []
        for step in range(1, n):
            copies.append(pltpu.make_async_remote_copy(
                src_ref=sums.at[me], dst_ref=sums.at[me],
                send_sem=send.at[step], recv_sem=recv.at[step],
                device_id={axis: lax.rem(me + step, n)}, device_id_type=MESH,
            ))
        for copy in copies:
            copy.start()
        for copy in copies:
            copy.wait()
        return jnp.sum(sums[...], 0)

    partial = reduce_over(partial, sums_y, send_y, recv_y, "ty", ty, n_y)
    partial = reduce_over(partial, sums_x, send_x, recv_x, "tx", tx, n_x)
    dots = jnp.sum(partial, 1, keepdims=True)
    rr, c01, s11, s02, s12 = (dots[k:k + 1] for k in range(5))
    alpha = rr / c01
    rr_next = rr - 2.0 * alpha * c01 + alpha * alpha * s11
    gain = 1.0 + rr_next / rr
    curvature = gain * gain * c01 - gain * alpha * (s02 + s11) + alpha * alpha * s12
    step_len = rr_next / curvature
    first = (alpha + step_len * gain) * SCALE
    second = step_len * alpha * SCALE
    for h in range(2):
        for t in range(2):
            out_ref[t, :, h * LANES:(h + 1) * LANES] = first * q0_ref[h, t] - second * q1_ref[h, t]


def sweep_kernel(first, group, corners, count, own, right, below, corner, probe, table_f, table_g, extra,
                 top, bottom, *rest):
    if first:
        psi_ref, turned, field, total = rest
    else:
        field, total = rest
        psi_ref, turned = extra, probe
    extent = probe.shape[-2]
    tile = own.shape[2]
    field[0:2, :, 0:tile] = own[...].astype(F32)
    field[2:4, :, 0:tile] = right[...].astype(F32)
    field[0:2, :, tile:] = below[...].astype(F32)
    field[2:4, :, tile:] = corner[...].astype(F32)
    total[...] = jnp.zeros_like(total)
    lane = lax.broadcasted_iota(jnp.int32, (extent, LANES), 1)
    live = count[0]

    def turn_probe(s):
        shift = lax.rem(corners[1, s], LANES)
        keep = lane >= shift
        for t in range(2):
            near = pltpu.roll(probe[t, :, 0:LANES], shift, 1)
            far = pltpu.roll(probe[t, :, LANES:], shift, 1)
            turned[s, t, :, 0:LANES] = jnp.where(keep, near, far)
            turned[s, t, :, LANES:] = jnp.where(keep, far, near)

    def cut(s):
        row, col = corners[0, s], corners[1, s]
        block, shift = col // LANES, lax.rem(col, LANES)
        keep = lane >= shift
        rows = pl.ds(row, extent)
        waves = [[], []]
        for k in range(2):
            halves = []
            for t in range(2):
                if k == 0:
                    halves.append(jnp.where(keep, field[block, t, rows, :], field[block + 2, t, rows, :]))
                else:
                    halves.append(field[block + 1, t, rows, :])
            lanes = slice(k * LANES, (k + 1) * LANES)
            probe_re, probe_im = turned[s, 0, :, lanes], turned[s, 1, :, lanes]
            waves[0].append((probe_re * halves[0] - probe_im * halves[1]).astype(BF16))
            waves[1].append((probe_re * halves[1] + probe_im * halves[0]).astype(BF16))
        return jnp.concatenate(waves[0] + waves[1], 1)

    def add(s, back):
        row, col = corners[0, s], corners[1, s]
        block, shift = col // LANES, lax.rem(col, LANES)
        keep = lane >= shift
        rows = pl.ds(row, extent)
        for k in range(2):
            lanes = slice(k * LANES, (k + 1) * LANES)
            probe_re, probe_im = turned[s, 0, :, lanes], turned[s, 1, :, lanes]
            re, im = back[:extent, lanes], back[extent:, lanes]
            for t in range(2):
                if t == 0:
                    term = probe_re * re + probe_im * im
                else:
                    term = probe_re * im - probe_im * re
                if k == 0:
                    zero = jnp.zeros_like(term)
                    total[block, t, rows, :] += jnp.where(keep, term, zero)
                    total[block + 2, t, rows, :] += jnp.where(keep, zero, term)
                else:
                    total[block + 1, t, rows, :] += term

    def transform(waves, rhs, lhs):
        half = jnp.dot(waves, rhs[...], preferred_element_type=F32).astype(BF16)
        columns = []
        for g in range(group):
            part = half[g * extent:(g + 1) * extent]
            columns.append(jnp.concatenate([part[:, :extent], part[:, extent:]], 0))
        return jnp.dot(lhs[...], jnp.concatenate(columns, 1), preferred_element_type=F32)

    def step(index, carry):
        base = index * group
        if first:
            for g in range(group):
                turn_probe(base + g)
        waves = jnp.concatenate([cut(base + g) for g in range(group)], 0)
        image = transform(waves, table_f, table_g)
        mixed = []
        for g in range(group):
            re = image[:extent, g * extent:(g + 1) * extent]
            im = image[extent:, g * extent:(g + 1) * extent]
            if first:
                psi_ref[base + g, 0] = re
                psi_ref[base + g, 1] = im
                weight = re * re + im * im - extra[base + g].astype(F32)
                psi_re, psi_im = re, im
            else:
                psi_re, psi_im = psi_ref[base + g, 0], psi_ref[base + g, 1]
                weight = psi_re * re + psi_im * im
            mixed.append(jnp.concatenate([(psi_re * weight).astype(BF16), (psi_im * weight).astype(BF16)], 1))
        back = transform(jnp.concatenate(mixed, 0), table_g, table_f)
        for g in range(group):
            @pl.when(base + g < live)
            def _():
                add(base + g, back[:, g * extent:(g + 1) * extent])
        return carry

    lax.fori_loop(0, (live + group - 1) // group, step, 0)
    top[...] = total[:, :, 0:tile]
    bottom[...] = total[:, :, tile:].astype(BF16)


def per_device(object_field, probe_field, corners, counts, intensity, damping):
    extent = probe_field.shape[-1]
    tile = object_field.shape[1]
    slots = corners.shape[2]
    group = min(4, slots)
    n_y, n_x = lax.axis_size("ty"), lax.axis_size("tx")
    places = corners.reshape(slots, 2).T
    count = counts.reshape(1)
    measured = intensity.reshape(slots, extent, extent)
    damping = damping.reshape(1)
    table_f, table_g = make_table(extent, -1.0), make_table(extent, 1.0)

    def shaped(shape, dtype):
        return jax.ShapeDtypeStruct(shape, dtype)

    quarter = (2, 2, tile, LANES)
    quarters = [shaped(quarter, BF16)] * 4
    boxes = [pltpu.VMEM(quarter, BF16)] * 4 + [pltpu.VMEM(quarter, F32)]

    def sems(n):
        return [pltpu.SemaphoreType.DMA((n,)), pltpu.SemaphoreType.DMA((n,))]

    def params(collective_id):
        return pltpu.CompilerParams(
            collective_id=collective_id, has_side_effects=True, vmem_limit_bytes=16 << 20
        )

    margins = pl.pallas_call(
        spread_kernel,
        out_shape=quarters,
        in_specs=[VMEM_SPEC],
        out_specs=[VMEM_SPEC] * 4,
        scratch_shapes=sems(3 * CHUNKS),
        compiler_params=params(0),
        cost_estimate=pl.CostEstimate(flops=10**10, bytes_accessed=30 << 20, transcendentals=0),
        name="spread",
    )(object_field)

    def sweep(margins, probe, extra, first):
        outs = [shaped((4, 2, tile, LANES), F32), shaped((4, 2, tile, LANES), BF16)]
        if first:
            outs += [shaped((slots, 2, extent, extent), F32)] * 2
        return pl.pallas_call(
            functools.partial(sweep_kernel, first, group),
            out_shape=outs,
            in_specs=[SMEM_SPEC] * 2 + [VMEM_SPEC] * 8,
            out_specs=[VMEM_SPEC] * len(outs),
            scratch_shapes=[pltpu.VMEM((4, 2, 2 * tile, LANES), F32)] * 2,
            compiler_params=pltpu.CompilerParams(vmem_limit_bytes=36 << 20),
            name="sweep_first" if first else "sweep",
        )(places, count, *margins, probe, table_f, table_g, extra)

    top, bottom, psi, turned = sweep(margins, probe_field, measured, True)
    q0, *margins = pl.pallas_call(
        functools.partial(exchange_kernel, True),
        out_shape=[shaped(quarter, F32)] + quarters,
        in_specs=[VMEM_SPEC] * 2,
        out_specs=[VMEM_SPEC] * 5,
        scratch_shapes=boxes + sems(6 * CHUNKS),
        compiler_params=params(1),
        name="exchange_first",
    )(top, bottom)
    top, bottom = sweep(margins, turned, psi, False)
    q1, *margins = pl.pallas_call(
        functools.partial(exchange_kernel, False),
        out_shape=[shaped(quarter, F32)] + quarters,
        in_specs=[SMEM_SPEC] + [VMEM_SPEC] * 3,
        out_specs=[VMEM_SPEC] * 5,
        scratch_shapes=boxes + sems(6 * CHUNKS),
        compiler_params=params(2),
        name="exchange",
    )(damping, top, bottom, q0)
    top, bottom = sweep(margins, turned, psi, False)
    return pl.pallas_call(
        finish_kernel,
        out_shape=shaped((2, tile, tile), F32),
        in_specs=[SMEM_SPEC] + [VMEM_SPEC] * 4,
        out_specs=VMEM_SPEC,
        scratch_shapes=boxes
        + [pltpu.VMEM((n_y, 8, LANES), F32), pltpu.VMEM((n_x, 8, LANES), F32)]
        + sems(3 * CHUNKS) + sems(n_y) + sems(n_x),
        compiler_params=params(3),
        name="finish",
    )(damping, top, bottom, q0, q1)


def solution(mesh):
    in_specs = (
        P(None, "ty", "tx"),
        P(),
        P("ty", "tx", None, None),
        P("ty", "tx"),
        P("ty", "tx", None, None, None),
        P(),
    )
    out_specs = P(None, "ty", "tx")
    return jax.shard_map(
        per_device, mesh=mesh, in_specs=in_specs, out_specs=out_specs, check_vma=False
    )
```

```python
import functools

import jax
import jax.numpy as jnp
import numpy as np
from jax import lax
from jax.experimental import pallas as pl
from jax.experimental.pallas import tpu as pltpu
from jax.sharding import PartitionSpec as P

MESH = pl.DeviceIdType.MESH
LANES = 128
SCALE = 2.0**-24
CHUNKS = 4
F32 = jnp.float32
BF16 = jnp.bfloat16
VMEM_SPEC = pl.BlockSpec(memory_space=pltpu.VMEM)
SMEM_SPEC = pl.BlockSpec(memory_space=pltpu.SMEM)


def make_table(extent, direction_sign):
    indices = np.arange(extent)
    angles = (indices[:, None] * indices[None, :] % extent) * (2.0 * np.pi / extent)
    cosine = np.cos(angles) / extent**0.5
    sines = direction_sign * np.sin(angles) / extent**0.5
    table = np.block([[cosine, sines], [-sines, cosine]])
    return jnp.asarray(table.astype(np.float32)).astype(BF16)


def place():
    ty, tx = lax.axis_index("ty"), lax.axis_index("tx")
    return ty, tx, ty > 0, ty < lax.axis_size("ty") - 1, tx > 0, tx < lax.axis_size("tx") - 1


def greet_neighbours():
    ty, tx, has_up, has_down, has_left, has_right = place()
    barrier = pltpu.get_barrier_semaphore()
    sides = (
        (has_up, {"ty": ty - 1}),
        (has_down, {"ty": ty + 1}),
        (has_left, {"tx": tx - 1}),
        (has_right, {"tx": tx + 1}),
    )
    for present, peer in sides:
        @pl.when(present)
        def _():
            pl.semaphore_signal(barrier, inc=1, device_id=peer, device_id_type=MESH)
    pl.semaphore_wait(barrier, sum(present.astype(jnp.int32) for present, _ in sides))


def remote(src, dst, send_sem, recv_sem, index, peer):
    return pltpu.make_async_remote_copy(
        src_ref=src,
        dst_ref=dst,
        send_sem=send_sem.at[index],
        recv_sem=recv_sem.at[index],
        device_id=peer,
        device_id_type=MESH,
    )


def rows_of(chunk, extent):
    size = extent // CHUNKS
    return pl.ds(chunk * size, size)


def margin_copies(out_left, in_right, own, right, below, corner, send_sem, recv_sem, base):
    ty, tx = place()[:2]
    to_left, to_up, on_up = [], [], []
    for c in range(CHUNKS):
        rows = rows_of(c, own.shape[2])
        part = [ref.at[:, :, rows] for ref in (out_left, in_right, own, right, below, corner)]
        to_left.append(remote(part[0], part[1], send_sem, recv_sem, base + 3 * c, {"tx": tx - 1}))
        to_up.append(remote(part[2], part[4], send_sem, recv_sem, base + 3 * c + 1, {"ty": ty - 1}))
        on_up.append(remote(part[3], part[5], send_sem, recv_sem, base + 3 * c + 2, {"ty": ty - 1}))
    return to_left, to_up, on_up


def start_if(present, copy):
    @pl.when(present)
    def _():
        copy.start()


def take_right(copies, c, on_arrival):
    ty, tx, has_up, has_down, has_left, has_right = place()

    @pl.when(has_right)
    def _():
        copies[0][c].wait_recv()
        on_arrival()

        @pl.when(has_up)
        def _():
            copies[2][c].start()


def settle_margins(copies):
    ty, tx, has_up, has_down, has_left, has_right = place()
    to_left, to_up, on_up = copies

    @pl.when(has_down)
    def _():
        for copy in to_up:
            copy.wait_recv()

        @pl.when(has_right)
        def _():
            for copy in on_up:
                copy.wait_recv()

    @pl.when(has_left)
    def _():
        for copy in to_left:
            copy.wait_send()

    @pl.when(has_up)
    def _():
        for copy in to_up:
            copy.wait_send()

        @pl.when(has_right)
        def _():
            for copy in on_up:
                copy.wait_send()


def fold_margins(top, bottom, inbox_far, inbox_near, outbox, inbox_side, total, beside, send_sem, recv_sem,
                 before_sum, after_sum):
    ty, tx, has_up, has_down, has_left, has_right = place()
    far, near, side, spans = [], [], [], []
    for c in range(CHUNKS):
        rows = rows_of(c, total.shape[2])
        spans.append(rows)
        far.append(remote(
            bottom.at[pl.ds(2, 2), :, rows], inbox_far.at[:, :, rows], send_sem, recv_sem, 3 * c, {"ty": ty + 1}
        ))
        near.append(remote(
            bottom.at[pl.ds(0, 2), :, rows], inbox_near.at[:, :, rows], send_sem, recv_sem, 3 * c + 1, {"ty": ty + 1}
        ))
        side.append(remote(
            outbox.at[:, :, rows], inbox_side.at[:, :, rows], send_sem, recv_sem, 3 * c + 2, {"tx": tx + 1}
        ))

    @pl.when(has_down)
    def _():
        for c in range(CHUNKS):
            far[c].start()
            near[c].start()

    for c in range(CHUNKS):
        rows = spans[c]

        @pl.when(has_up)
        def _():
            far[c].wait_recv()
            near[c].wait_recv()
            beside[:, :, rows] = top[2:4, :, rows] + inbox_far[:, :, rows].astype(F32)
            total[:, :, rows] = top[0:2, :, rows] + inbox_near[:, :, rows].astype(F32)

        @pl.when(ty == 0)
        def _():
            beside[:, :, rows] = top[2:4, :, rows]
            total[:, :, rows] = top[0:2, :, rows]

        @pl.when(has_right)
        def _():
            outbox[:, :, rows] = beside[:, :, rows].astype(BF16)
            side[c].start()

        before_sum(c, rows)

    for c in range(CHUNKS):
        @pl.when(has_left)
        def _():
            side[c].wait_recv()
            total[:, :, spans[c]] += inbox_side[:, :, spans[c]].astype(F32)

        after_sum(c, spans[c])

    @pl.when(has_down)
    def _():
        for copy in far + near:
            copy.wait_send()

    @pl.when(has_right)
    def _():
        for copy in side:
            copy.wait_send()


def spread_kernel(object_ref, own, right, below, corner, send_sem, recv_sem):
    for h in range(2):
        for t in range(2):
            own[h, t] = object_ref[t, :, h * LANES:(h + 1) * LANES]
    greet_neighbours()
    copies = margin_copies(own, right, own, right, below, corner, send_sem, recv_sem, 0)
    has_up, has_left = place()[2], place()[4]
    for c in range(CHUNKS):
        start_if(has_left, copies[0][c])
        start_if(has_up, copies[1][c])
    for c in range(CHUNKS):
        take_right(copies, c, lambda: None)
    settle_margins(copies)


def exchange_kernel(first, *refs):
    if first:
        top, bottom = refs[:2]
        refs = refs[2:]
    else:
        damping, top, bottom, before, before_right = refs[:5]
        refs = refs[5:]
    q_ref, q_right, own, right, below, corner = refs[:6]
    boxes, (out_left, in_right, send_sem, recv_sem) = refs[6:12], refs[12:]
    total, beside = boxes[-2:]
    has_up, has_left = place()[2], place()[4]
    greet_neighbours()
    copies = margin_copies(out_left, in_right, own, right, below, corner, send_sem, recv_sem, 3 * CHUNKS)

    def scaled(sums, old, rows):
        if first:
            return -2.0 * sums
        return (4.0 * SCALE) * sums + (damping[0] * SCALE) * old[:, :, rows]

    def send_part(c, rows):
        @pl.when(has_left)
        def _():
            out_left[:, :, rows] = total[:, :, rows].astype(BF16)
            copies[0][c].start()

    def use(c, rows):
        q = scaled(total[:, :, rows], None if first else before, rows)
        q_ref[:, :, rows] = q
        own[:, :, rows] = q.astype(BF16)
        start_if(has_up, copies[1][c])

        def on_arrival():
            sums = beside[:, :, rows] + in_right[:, :, rows].astype(F32)
            q = scaled(sums, None if first else before_right, rows)
            q_right[:, :, rows] = q
            right[:, :, rows] = q.astype(BF16)

        take_right(copies, c, on_arrival)

    fold_margins(top, bottom, *boxes, send_sem, recv_sem, send_part, use)
    settle_margins(copies)


def lane_sums(values):
    return jnp.sum(values.reshape(-1, LANES), 0, keepdims=True)


def finish_kernel(damping, top, bottom, q0_ref, q1_ref, out_ref,
                  inbox_far, inbox_near, outbox, inbox_side, total, beside, sums_y, sums_x,
                  send_sem, recv_sem, send_y, recv_y, send_x, recv_x):
    ty, tx, has_up, has_down, has_left, has_right = place()
    n_y, n_x = lax.axis_size("ty"), lax.axis_size("tx")
    barrier = pltpu.get_barrier_semaphore()
    for axis, me, n in (("ty", ty, n_y), ("tx", tx, n_x)):
        for step in range(1, n):
            pl.semaphore_signal(
                barrier, inc=1, device_id={axis: lax.rem(me + step, n)}, device_id_type=MESH
            )
    pl.semaphore_wait(barrier, n_y + n_x - 2)
    fold_margins(top, bottom, inbox_far, inbox_near, outbox, inbox_side, total, beside, send_sem, recv_sem,
                 lambda c, rows: None, lambda c, rows: None)
    q0, q1 = q0_ref[...], q1_ref[...]
    q2 = (4.0 * SCALE) * total[...] + (damping[0] * SCALE) * q1
    rows = [lane_sums(q0 * q0), lane_sums(q0 * q1), lane_sums(q1 * q1), lane_sums(q0 * q2), lane_sums(q1 * q2)]
    partial = jnp.concatenate(rows + [jnp.zeros((3, LANES), F32)], 0)

    def reduce_over(partial, sums, send, recv, axis, me, n):
        sums[me] = partial
        copies = []
        for step in range(1, n):
            copies.append(pltpu.make_async_remote_copy(
                src_ref=sums.at[me], dst_ref=sums.at[me],
                send_sem=send.at[step], recv_sem=recv.at[step],
                device_id={axis: lax.rem(me + step, n)}, device_id_type=MESH,
            ))
        for copy in copies:
            copy.start()
        for copy in copies:
            copy.wait()
        return jnp.sum(sums[...], 0)

    partial = reduce_over(partial, sums_y, send_y, recv_y, "ty", ty, n_y)
    partial = reduce_over(partial, sums_x, send_x, recv_x, "tx", tx, n_x)
    dots = jnp.sum(partial, 1, keepdims=True)
    rr, c01, s11, s02, s12 = (dots[k:k + 1] for k in range(5))
    alpha = rr / c01
    rr_next = rr - 2.0 * alpha * c01 + alpha * alpha * s11
    gain = 1.0 + rr_next / rr
    curvature = gain * gain * c01 - gain * alpha * (s02 + s11) + alpha * alpha * s12
    step_len = rr_next / curvature
    first = (alpha + step_len * gain) * SCALE
    second = step_len * alpha * SCALE
    for h in range(2):
        for t in range(2):
            out_ref[t, :, h * LANES:(h + 1) * LANES] = first * q0_ref[h, t] - second * q1_ref[h, t]


def sweep_kernel(first, group, corners, count, own, right, below, corner, probe, table_f, table_g, extra,
                 top, bottom, *rest):
    if first:
        psi_ref, turned, field, total = rest
    else:
        field, total = rest
        psi_ref, turned = extra, probe
    extent = probe.shape[-2]
    tile = own.shape[2]
    field[0:2, :, 0:tile] = own[...].astype(F32)
    field[2:4, :, 0:tile] = right[...].astype(F32)
    field[0:2, :, tile:] = below[...].astype(F32)
    field[2:4, :, tile:] = corner[...].astype(F32)
    total[...] = jnp.zeros_like(total)
    lane = lax.broadcasted_iota(jnp.int32, (extent, LANES), 1)
    live = count[0]

    def turn_probe(s):
        shift = lax.rem(corners[1, s], LANES)
        keep = lane >= shift
        for t in range(2):
            near = pltpu.roll(probe[t, :, 0:LANES], shift, 1)
            far = pltpu.roll(probe[t, :, LANES:], shift, 1)
            turned[s, t, :, 0:LANES] = jnp.where(keep, near, far)
            turned[s, t, :, LANES:] = jnp.where(keep, far, near)

    def cut(s):
        row, col = corners[0, s], corners[1, s]
        block, shift = col // LANES, lax.rem(col, LANES)
        keep = lane >= shift
        rows = pl.ds(row, extent)
        waves = [[], []]
        for k in range(2):
            halves = []
            for t in range(2):
                if k == 0:
                    halves.append(jnp.where(keep, field[block, t, rows, :], field[block + 2, t, rows, :]))
                else:
                    halves.append(field[block + 1, t, rows, :])
            lanes = slice(k * LANES, (k + 1) * LANES)
            probe_re, probe_im = turned[s, 0, :, lanes], turned[s, 1, :, lanes]
            waves[0].append((probe_re * halves[0] - probe_im * halves[1]).astype(BF16))
            waves[1].append((probe_re * halves[1] + probe_im * halves[0]).astype(BF16))
        return jnp.concatenate(waves[0] + waves[1], 1)

    def add(s, back):
        row, col = corners[0, s], corners[1, s]
        block, shift = col // LANES, lax.rem(col, LANES)
        keep = lane >= shift
        rows = pl.ds(row, extent)
        for k in range(2):
            lanes = slice(k * LANES, (k + 1) * LANES)
            probe_re, probe_im = turned[s, 0, :, lanes], turned[s, 1, :, lanes]
            re, im = back[:extent, lanes], back[extent:, lanes]
            for t in range(2):
                if t == 0:
                    term = probe_re * re + probe_im * im
                else:
                    term = probe_re * im - probe_im * re
                if k == 0:
                    zero = jnp.zeros_like(term)
                    total[block, t, rows, :] += jnp.where(keep, term, zero)
                    total[block + 2, t, rows, :] += jnp.where(keep, zero, term)
                else:
                    total[block + 1, t, rows, :] += term

    def transform(waves, rhs, lhs):
        half = jnp.dot(waves, rhs[...], preferred_element_type=F32).astype(BF16)
        columns = []
        for g in range(group):
            part = half[g * extent:(g + 1) * extent]
            columns.append(jnp.concatenate([part[:, :extent], part[:, extent:]], 0))
        return jnp.dot(lhs[...], jnp.concatenate(columns, 1), preferred_element_type=F32)

    def step(index, carry):
        base = index * group
        if first:
            for g in range(group):
                turn_probe(base + g)
        waves = jnp.concatenate([cut(base + g) for g in range(group)], 0)
        image = transform(waves, table_f, table_g)
        mixed = []
        for g in range(group):
            re = image[:extent, g * extent:(g + 1) * extent]
            im = image[extent:, g * extent:(g + 1) * extent]
            if first:
                psi_ref[base + g, 0] = re
                psi_ref[base + g, 1] = im
                weight = re * re + im * im - extra[base + g].astype(F32)
                psi_re, psi_im = re, im
            else:
                psi_re, psi_im = psi_ref[base + g, 0], psi_ref[base + g, 1]
                weight = psi_re * re + psi_im * im
            mixed.append(jnp.concatenate([(psi_re * weight).astype(BF16), (psi_im * weight).astype(BF16)], 1))
        back = transform(jnp.concatenate(mixed, 0), table_g, table_f)
        for g in range(group):
            @pl.when(base + g < live)
            def _():
                add(base + g, back[:, g * extent:(g + 1) * extent])
        return carry

    lax.fori_loop(0, (live + group - 1) // group, step, 0)
    top[...] = total[:, :, 0:tile]
    bottom[...] = total[:, :, tile:].astype(BF16)


def per_device(object_field, probe_field, corners, counts, intensity, damping):
    extent = probe_field.shape[-1]
    tile = object_field.shape[1]
    slots = corners.shape[2]
    group = min(4, slots)
    n_y, n_x = lax.axis_size("ty"), lax.axis_size("tx")
    places = corners.reshape(slots, 2).T
    count = counts.reshape(1)
    measured = intensity.reshape(slots, extent, extent)
    damping = damping.reshape(1)
    table_f, table_g = make_table(extent, -1.0), make_table(extent, 1.0)

    def shaped(shape, dtype):
        return jax.ShapeDtypeStruct(shape, dtype)

    quarter = (2, 2, tile, LANES)
    quarters = [shaped(quarter, BF16)] * 4
    boxes = [pltpu.VMEM(quarter, BF16)] * 4 + [pltpu.VMEM(quarter, F32)] * 2

    def sems(n):
        return [pltpu.SemaphoreType.DMA((n,)), pltpu.SemaphoreType.DMA((n,))]

    def params(collective_id):
        return pltpu.CompilerParams(
            collective_id=collective_id, has_side_effects=True, vmem_limit_bytes=16 << 20
        )

    margins = pl.pallas_call(
        spread_kernel,
        out_shape=quarters,
        in_specs=[VMEM_SPEC],
        out_specs=[VMEM_SPEC] * 4,
        scratch_shapes=sems(3 * CHUNKS),
        compiler_params=params(0),
        cost_estimate=pl.CostEstimate(flops=10**10, bytes_accessed=30 << 20, transcendentals=0),
        name="spread",
    )(object_field)

    def sweep(margins, probe, extra, first):
        outs = [shaped((4, 2, tile, LANES), F32), shaped((4, 2, tile, LANES), BF16)]
        if first:
            outs += [shaped((slots, 2, extent, extent), F32)] * 2
        return pl.pallas_call(
            functools.partial(sweep_kernel, first, group),
            out_shape=outs,
            in_specs=[SMEM_SPEC] * 2 + [VMEM_SPEC] * 8,
            out_specs=[VMEM_SPEC] * len(outs),
            scratch_shapes=[pltpu.VMEM((4, 2, 2 * tile, LANES), F32)] * 2,
            compiler_params=pltpu.CompilerParams(vmem_limit_bytes=36 << 20),
            name="sweep_first" if first else "sweep",
        )(places, count, *margins, probe, table_f, table_g, extra)

    top, bottom, psi, turned = sweep(margins, probe_field, measured, True)
    q0, q0_right, *margins = pl.pallas_call(
        functools.partial(exchange_kernel, True),
        out_shape=[shaped(quarter, F32)] * 2 + quarters,
        in_specs=[VMEM_SPEC] * 2,
        out_specs=[VMEM_SPEC] * 6,
        scratch_shapes=boxes + [pltpu.VMEM(quarter, BF16)] * 2 + sems(6 * CHUNKS),
        compiler_params=params(1),
        name="exchange_first",
    )(top, bottom)
    top, bottom = sweep(margins, turned, psi, False)
    q1, _, *margins = pl.pallas_call(
        functools.partial(exchange_kernel, False),
        out_shape=[shaped(quarter, F32)] * 2 + quarters,
        in_specs=[SMEM_SPEC] + [VMEM_SPEC] * 4,
        out_specs=[VMEM_SPEC] * 6,
        scratch_shapes=boxes + [pltpu.VMEM(quarter, BF16)] * 2 + sems(6 * CHUNKS),
        compiler_params=params(2),
        name="exchange",
    )(damping, top, bottom, q0, q0_right)
    top, bottom = sweep(margins, turned, psi, False)
    return pl.pallas_call(
        finish_kernel,
        out_shape=shaped((2, tile, tile), F32),
        in_specs=[SMEM_SPEC] + [VMEM_SPEC] * 4,
        out_specs=VMEM_SPEC,
        scratch_shapes=boxes
        + [pltpu.VMEM((n_y, 8, LANES), F32), pltpu.VMEM((n_x, 8, LANES), F32)]
        + sems(3 * CHUNKS) + sems(n_y) + sems(n_x),
        compiler_params=params(3),
        name="finish",
    )(damping, top, bottom, q0, q1)


def solution(mesh):
    in_specs = (
        P(None, "ty", "tx"),
        P(),
        P("ty", "tx", None, None),
        P("ty", "tx"),
        P("ty", "tx", None, None, None),
        P(),
    )
    out_specs = P(None, "ty", "tx")
    return jax.shard_map(
        per_device, mesh=mesh, in_specs=in_specs, out_specs=out_specs, check_vma=False
    )
```
